256 devices in a mesh: group: 4 (over y), dev: 64 (over z, x, core).
Axes of the slice: x: 4, y: 4, z: 8, core: 2. Of those that a mesh axis runs over, the one named last changes fastest.
Arguments:
- embeddings: bfloat16 [524288, 1024], P(('group', 'dev')), may hold values from -6 to 6
- pair_blocks: int32 [4096, 2], P(('group', 'dev')), may hold values from -1 to 2047, as said below
- pair_count: int32 [256], P(('group', 'dev')), may hold values from 0 to 16, as said below
Outputs:
- smoothed: bfloat16 [524288, 1024], P(('group', 'dev'))
The draws below stay inside these ranges and needn't reach their ends.
Inputs may be any that keep to these rules, and one draw needn't show every extreme that they name: `pair_blocks`: A used slot holds two global block numbers (left, right): left is a block of the slot's device; right is another block of that device, a block of the device with the next dev index in the same group, or a block of the device with the same dev index in the next group. No unordered pair of blocks is listed twice. Unused slots hold -1 in both places. `pair_count`: some device uses all 16 of its slots.
All inputs are finite; a program needn't handle non-finite values.
Results may differ from the reference program's by a relative error of at most 0.003.
Values may be sent and summed in bfloat16 or wider, within the bound.
A program may use at most 128 MiB of HBM per device.

```python
import math
import jax
import jax.numpy as jnp
import numpy as np
from jax import lax

D = 1024
BLOCK = 256
BLK_DEV = 8
PAIR_DEV = 16
GROUPS = 4
OWNERS = 64
NBLK = 2048
ROWS = 524288


def draw_embeddings(key, part):
    total_blocks = BLK_DEV * GROUPS * OWNERS
    total_rows = total_blocks * BLOCK
    clusters = (total_blocks + 1) // 2
    latent_count = max(D // 8, 8)
    column_latent = jax.random.randint(jax.random.fold_in(key, 14), (D,), 0, latent_count)
    column_scale = jnp.exp(jax.random.uniform(jax.random.fold_in(key, 15), (D,), jnp.float32, math.log(0.7), math.log(1.3)))
    centers = 0.5 * jax.random.normal(jax.random.fold_in(key, 11), (clusters, latent_count), jnp.float32)
    within = jax.random.normal(jax.random.fold_in(key, 16), (total_rows, latent_count), jnp.float32)
    noise = 0.4 * jax.random.normal(jax.random.fold_in(key, 12), (total_rows, D), jnp.float32)
    row_cluster = jnp.arange(total_rows) // (2 * BLOCK)
    latent = jnp.take(centers, row_cluster, axis=0) + within
    spread = jnp.take(latent, column_latent, axis=1) * column_scale[None, :]
    values = spread + noise
    return jnp.clip(values, -6.0, 6.0).astype(jnp.bfloat16)


def pair_table(key):
    left_list = []
    right_list = []
    kind_list = []
    for first_idx in range(BLK_DEV):
        for second_idx in range(first_idx + 1, BLK_DEV):
            left_list.append(first_idx)
            right_list.append(second_idx)
            kind_list.append(0)
    for first_idx in range(BLK_DEV):
        for second_idx in range(BLK_DEV):
            left_list.append(first_idx)
            right_list.append(BLK_DEV + second_idx)
            kind_list.append(1)
            left_list.append(first_idx)
            right_list.append(2 * BLK_DEV + second_idx)
            kind_list.append(2)
    cand_left = jnp.asarray(np.array(left_list, dtype=np.int32))
    cand_right = jnp.asarray(np.array(right_list, dtype=np.int32))
    cand_kind = jnp.asarray(np.array(kind_list, dtype=np.int32))
    candidates = len(left_list)
    devices = GROUPS * OWNERS
    base = jax.random.fold_in(key, 5)
    scores = jax.random.randint(jax.random.fold_in(base, 1), (devices, candidates), 0, 1 << 20) * candidates
    scores = scores + jnp.arange(candidates, dtype=jnp.int32)[None, :]
    device_ids = jnp.arange(devices, dtype=jnp.int32)[:, None]
    group_ids = device_ids // OWNERS
    owner_ids = device_ids % OWNERS
    invalid = (cand_kind[None, :] == 1) & (owner_ids == OWNERS - 1) | (cand_kind[None, :] == 2) & (group_ids == GROUPS - 1)
    scores = scores + invalid.astype(jnp.int32) * (1 << 29)
    order = jnp.argsort(scores, axis=1)[:, :PAIR_DEV]
    valid_count = jnp.sum(jnp.logical_not(invalid).astype(jnp.int32), axis=1)
    drawn = jax.random.randint(jax.random.fold_in(base, 2), (devices,), PAIR_DEV // 4, PAIR_DEV + 1)
    full_group = jax.random.randint(jax.random.fold_in(base, 3), (), 0, GROUPS - 1)
    full_owner = jax.random.randint(jax.random.fold_in(base, 4), (), 0, OWNERS - 1)
    full_device = full_group * OWNERS + full_owner
    drawn = jnp.where(jnp.arange(devices) == full_device, PAIR_DEV, drawn)
    counts = jnp.minimum(drawn, valid_count).astype(jnp.int32)
    first_block = device_ids * BLK_DEV
    left_code = cand_left[order]
    right_code = cand_right[order]
    left_global = first_block + left_code
    right_global = jnp.where(right_code < 2 * BLK_DEV, first_block + right_code, first_block + OWNERS * BLK_DEV + right_code - 2 * BLK_DEV)
    used = jnp.arange(PAIR_DEV, dtype=jnp.int32)[None, :] < counts[:, None]
    pairs = jnp.stack([jnp.where(used, left_global, -1), jnp.where(used, right_global, -1)], axis=-1)
    return (pairs.reshape(devices * PAIR_DEV, 2).astype(jnp.int32), counts)


def draw_pair_blocks(key, part):
    return pair_table(key)[0]


def draw_pair_count(key, part):
    return pair_table(key)[1]


def setup_inputs(seed: int = 0) -> dict:
    splits = jax.random.split(jax.random.key(seed), 4)
    return {
        "embeddings": draw_embeddings(jax.random.fold_in(splits[3], 71), 0),
        "pair_blocks": draw_pair_blocks(jax.random.fold_in(splits[3], 71), 0),
        "pair_count": draw_pair_count(jax.random.fold_in(splits[3], 71), 0),
    }


def kernel_tile(left_rows, right_rows, left_sq, right_sq):
    inner = jnp.dot(left_rows, right_rows.T, preferred_element_type=jnp.float32)
    distance = left_sq[:, None] + right_sq[None, :] - 2.0 * inner
    return jnp.exp(-distance / (0.4 * left_rows.shape[1])).astype(jnp.bfloat16)


def reference(embeddings, pair_blocks, pair_count):
    blocks = embeddings.reshape(NBLK, BLOCK, D)
    widened = blocks.astype(jnp.float32)
    squares = jnp.sum(widened * widened, axis=2)

    def diagonal(items):
        own_rows, own_sq = items
        weights = kernel_tile(own_rows, own_rows, own_sq, own_sq)
        return (jnp.dot(weights, own_rows, preferred_element_type=jnp.float32),
                jnp.sum(weights.astype(jnp.float32), axis=1))

    numer, denom = lax.map(diagonal, (blocks, squares))
    slot_count = pair_blocks.shape[0]
    per_device = slot_count // pair_count.shape[0]
    positions = jnp.arange(slot_count, dtype=jnp.int32)
    used = (positions % per_device) < pair_count[positions // per_device]

    def each_pair(totals, items):
        numer_acc, denom_acc = totals
        pair_ids, flag = items
        left_idx = jnp.maximum(pair_ids[0], 0).astype(jnp.int32)
        right_idx = jnp.maximum(pair_ids[1], 0).astype(jnp.int32)
        left_rows = blocks[left_idx]
        right_rows = blocks[right_idx]
        weights = kernel_tile(left_rows, right_rows, squares[left_idx], squares[right_idx])
        weights = weights * flag.astype(weights.dtype)
        wide_weights = weights.astype(jnp.float32)
        numer_acc = numer_acc.at[left_idx].add(jnp.dot(weights, right_rows, preferred_element_type=jnp.float32))
        denom_acc = denom_acc.at[left_idx].add(jnp.sum(wide_weights, axis=1))
        numer_acc = numer_acc.at[right_idx].add(jnp.dot(weights.T, left_rows, preferred_element_type=jnp.float32))
        denom_acc = denom_acc.at[right_idx].add(jnp.sum(wide_weights, axis=0))
        return (numer_acc, denom_acc), None

    (numer, denom), _ = lax.scan(each_pair, (numer, denom), (pair_blocks, used))
    smoothed = (numer / denom[:, :, None]).astype(jnp.bfloat16)
    return smoothed.reshape(ROWS, D)
```

```python
import jax
import jax.numpy as jnp
from jax import lax
from jax.experimental import pallas as pl
from jax.experimental.pallas import tpu as pltpu
from jax.sharding import PartitionSpec as P

BLOCK = 256
scale_factor = 0.4

C_T, C_SRC, C_PROW, C_VALID, C_FIRST, C_LAST, C_IDX = 0, 1, 2, 3, 4, 5, 6
NSRC = 5
NCOL = 16


def shifted(shard, axis, by):
    devices = lax.axis_size(axis)
    pairs = [(i, i + by) for i in range(devices) if 0 <= i + by < devices]
    return lax.ppermute(shard, axis, pairs)


def squares_of(blocks):
    return jnp.einsum("bsd,bsd->bs", blocks, blocks, preferred_element_type=jnp.float32)


def build_table(own_pairs, own_count, pd_pairs, pd_count, pg_pairs, pg_count,
                first_block, nloc, owners):
    slots = own_pairs.shape[0]
    pos = jnp.arange(slots, dtype=jnp.int32)

    def locate(g):
        off = g - first_block
        src = jnp.where(off < nloc, 0, jnp.where(off < 2 * nloc, 1, 2))
        idx = jnp.where(off < nloc, off, jnp.where(off < 2 * nloc, off - nloc,
                                                   g - first_block - owners * nloc))
        return src, idx

    used = pos < own_count[0]
    left = own_pairs[:, 0] - first_block
    rsrc, ridx = locate(own_pairs[:, 1])
    t_list = [jnp.arange(nloc, dtype=jnp.int32)]
    s_list = [jnp.zeros((nloc,), jnp.int32)]
    i_list = [jnp.arange(nloc, dtype=jnp.int32)]
    v_list = [jnp.ones((nloc,), bool)]
    t_list.append(left); s_list.append(rsrc); i_list.append(ridx); v_list.append(used)
    t_list.append(ridx); s_list.append(jnp.zeros_like(left)); i_list.append(left)
    v_list.append(used & (rsrc == 0))
    for src, pairs, count, prev_first in ((3, pd_pairs, pd_count, first_block - nloc),
                                          (4, pg_pairs, pg_count, first_block - owners * nloc)):
        u = pos < count[0]
        r = pairs[:, 1] - first_block
        u = u & (r >= 0) & (r < nloc)
        t_list.append(r); s_list.append(jnp.full_like(r, src))
        i_list.append(pairs[:, 0] - prev_first); v_list.append(u)
    t = jnp.concatenate(t_list)
    s = jnp.concatenate(s_list)
    ix = jnp.concatenate(i_list)
    v = jnp.concatenate(v_list)
    n = t.shape[0]
    t = jnp.where(v, jnp.clip(t, 0, nloc - 1), nloc)
    ix = jnp.clip(ix, 0, nloc - 1)
    order = jnp.argsort(t * n + jnp.arange(n, dtype=jnp.int32))
    t, s, ix, v = t[order], s[order], ix[order], v[order]
    t = jnp.where(v, t, nloc - 1)
    prev_t = jnp.concatenate([jnp.full((1,), -1, jnp.int32), t[:-1]])
    next_t = jnp.concatenate([t[1:], jnp.full((1,), -1, jnp.int32)])
    next_v = jnp.concatenate([v[1:], jnp.zeros((1,), bool)])
    first = v & (t != prev_t)
    last = v & ((t != next_t) | ~next_v)
    steps = jnp.arange(n, dtype=jnp.int32)
    cols = [t, s, s * nloc + ix, v.astype(jnp.int32), first.astype(jnp.int32),
            last.astype(jnp.int32)]
    for src in range(NSRC):
        active = v & (s == src)
        last_pos = lax.cummax(jnp.where(active, steps, -1))
        first_idx = ix[jnp.argmax(active)]
        cols.append(jnp.where(last_pos >= 0, ix[jnp.maximum(last_pos, 0)], first_idx))
    while len(cols) < NCOL:
        cols.append(jnp.zeros_like(t))
    return jnp.stack(cols, axis=1).reshape(-1).astype(jnp.int32), n


def smooth_kernel(tab, xt_ref, sqc_ref, p0, p1, p2, p3, p4, sqr_ref, out_ref, num_acc, den_acc):
    i = pl.program_id(0)
    base = i * NCOL
    valid = tab[base + C_VALID] == 1
    src = tab[base + C_SRC]
    prow = tab[base + C_PROW]
    width = xt_ref.shape[2]

    @pl.when(tab[base + C_FIRST] == 1)
    def _():
        num_acc[...] = jnp.zeros_like(num_acc)
        den_acc[...] = jnp.zeros_like(den_acc)

    def contribute(p_ref):
        xt = xt_ref[0]
        xp = p_ref[0]
        inner = lax.dot_general(xt, xp, (((1,), (1,)), ((), ())),
                                preferred_element_type=jnp.float32)
        sq_t = sqc_ref[0]
        sq_p = sqr_ref[pl.ds(prow, 1), :]
        distance = sq_t + sq_p - 2.0 * inner
        w = jnp.exp(-distance / (scale_factor * width)).astype(jnp.bfloat16)
        num_acc[...] += jnp.dot(w, xp, preferred_element_type=jnp.float32)
        den_acc[...] += jnp.sum(w.astype(jnp.float32), axis=1, keepdims=True)

    for k, p_ref in enumerate((p0, p1, p2, p3, p4)):
        @pl.when(valid & (src == k))
        def _():
            contribute(p_ref)

    @pl.when(tab[base + C_LAST] == 1)
    def _():
        out_ref[0] = (num_acc[...] / den_acc[...]).astype(out_ref.dtype)


def local(embeddings, pair_blocks, pair_count):
    total_rows, width = embeddings.shape
    nloc = total_rows // BLOCK
    blocks = embeddings.reshape(nloc, BLOCK, width)
    own_sq = squares_of(blocks)
    owners = lax.axis_size("dev")
    first_block = (lax.axis_index("group") * owners + lax.axis_index("dev")) * nloc

    nd = shifted(blocks, "dev", -1)
    ng = shifted(blocks, "group", -1)
    pd = shifted(blocks, "dev", 1)
    pg = shifted(blocks, "group", 1)
    sq_all = jnp.concatenate([own_sq, shifted(own_sq, "dev", -1), shifted(own_sq, "group", -1),
                              shifted(own_sq, "dev", 1), shifted(own_sq, "group", 1)], axis=0)
    pd_pairs = shifted(pair_blocks, "dev", 1)
    pd_count = shifted(pair_count, "dev", 1)
    pg_pairs = shifted(pair_blocks, "group", 1)
    pg_count = shifted(pair_count, "group", 1)

    tab, steps = build_table(pair_blocks, pair_count, pd_pairs, pd_count, pg_pairs, pg_count,
                             first_block, nloc, owners)
    sq_col = own_sq[:, :, None]

    blk = (1, BLOCK, width)

    def t_map(i, tab):
        return (tab[i * NCOL + C_T], 0, 0)

    def src_map(k):
        def m(i, tab):
            return (tab[i * NCOL + C_IDX + k], 0, 0)
        return m

    grid_spec = pltpu.PrefetchScalarGridSpec(
        num_scalar_prefetch=1,
        grid=(steps,),
        in_specs=[pl.BlockSpec(blk, t_map),
                  pl.BlockSpec((1, BLOCK, 1), t_map)]
        + [pl.BlockSpec(blk, src_map(k)) for k in range(NSRC)]
        + [pl.BlockSpec(memory_space=pltpu.VMEM)],
        out_specs=pl.BlockSpec(blk, t_map),
        scratch_shapes=[pltpu.VMEM((BLOCK, width), jnp.float32),
                        pltpu.VMEM((BLOCK, 1), jnp.float32)],
    )
    flops = steps * 4 * BLOCK * BLOCK * width
    smoothed = pl.pallas_call(
        smooth_kernel,
        grid_spec=grid_spec,
        out_shape=jax.ShapeDtypeStruct((nloc, BLOCK, width), jnp.bfloat16),
        compiler_params=pltpu.CompilerParams(dimension_semantics=("arbitrary",)),
        cost_estimate=pl.CostEstimate(flops=flops, transcendentals=steps * BLOCK * BLOCK,
                                      bytes_accessed=steps * BLOCK * width * 2 * 2),
    )(tab, blocks, sq_col, blocks, nd, ng, pd, pg, sq_all)
    return smoothed.reshape(total_rows, width)


def solution(mesh):
    placed = (P(("group", "dev"), None), P(("group", "dev"), None), P(("group", "dev")))
    return jax.shard_map(
        local, mesh=mesh, in_specs=placed, out_specs=P(("group", "dev"), None), check_vma=False
    )
```

```python
import jax
import jax.numpy as jnp
from jax import lax
from jax.experimental import pallas as pl
from jax.experimental.pallas import tpu as pltpu
from jax.sharding import PartitionSpec as P

BLOCK = 256
scale_factor = 0.4

C_T, C_SRC, C_PROW, C_COMP, C_FIRST, C_LAST, C_IDX = 0, 1, 2, 3, 4, 5, 6
NCOL = 8


def shifted(shard, axis, by):
    devices = lax.axis_size(axis)
    pairs = [(i, i + by) for i in range(devices) if 0 <= i + by < devices]
    return lax.ppermute(shard, axis, pairs)


def squares_of(blocks):
    return jnp.einsum("bsd,bsd->bs", blocks, blocks, preferred_element_type=jnp.float32)


def order_table(t, s, ix, comp, valid, nloc, nsrc):
    n = t.shape[0]
    key = jnp.where(valid, jnp.clip(t, 0, nloc - 1), nloc)
    order = jnp.argsort(key * n + jnp.arange(n, dtype=jnp.int32))
    t, s, ix, comp, valid = t[order], s[order], ix[order], comp[order], valid[order]
    t = jnp.where(valid, jnp.clip(t, 0, nloc - 1), nloc - 1)
    ix = jnp.clip(ix, 0, nloc - 1)
    comp = comp & valid
    prev_t = jnp.concatenate([jnp.full((1,), -1, jnp.int32), t[:-1]])
    next_t = jnp.concatenate([t[1:], jnp.full((1,), -1, jnp.int32)])
    next_v = jnp.concatenate([valid[1:], jnp.zeros((1,), bool)])
    first = valid & (t != prev_t)
    last = valid & ((t != next_t) | ~next_v)
    steps = jnp.arange(n, dtype=jnp.int32)
    s = jnp.clip(s, 0, nsrc - 1)
    cols = [t, s, s * nloc + ix, comp.astype(jnp.int32), first.astype(jnp.int32),
            last.astype(jnp.int32)]
    for src in range(nsrc):
        active = comp & (s == src)
        last_pos = lax.cummax(jnp.where(active, steps, -1))
        first_idx = ix[jnp.argmax(active)]
        cols.append(jnp.where(last_pos >= 0, ix[jnp.maximum(last_pos, 0)], first_idx))
    while len(cols) < NCOL:
        cols.append(jnp.zeros_like(t))
    return jnp.stack(cols, axis=1).reshape(-1).astype(jnp.int32), n


def make_kernel(nsrc, mode):
    def kernel(tab, *refs):
        if mode == "init":
            xt_ref, sqc_ref = refs[:2]
            p_refs = refs[2:2 + nsrc]
            sqr_ref = refs[2 + nsrc]
            num_out, den_out, num_acc, den_acc = refs[3 + nsrc:]
        else:
            xt_ref, sqc_ref = refs[:2]
            p_refs = refs[2:2 + nsrc]
            sqr_ref, num_in, den_in = refs[2 + nsrc:5 + nsrc]
            outs = refs[5 + nsrc:]
            num_acc, den_acc = outs[-2:]
        i = pl.program_id(0)
        base = i * NCOL
        comp = tab[base + C_COMP] == 1
        src = tab[base + C_SRC]
        prow = tab[base + C_PROW]
        width = xt_ref.shape[2]

        @pl.when(tab[base + C_FIRST] == 1)
        def _():
            if mode == "init":
                num_acc[...] = jnp.zeros_like(num_acc)
                den_acc[...] = jnp.zeros_like(den_acc)
            else:
                num_acc[...] = num_in[0]
                den_acc[...] = den_in[0]

        def contribute(p_ref):
            xt = xt_ref[0]
            xp = p_ref[0]
            inner = lax.dot_general(xt, xp, (((1,), (1,)), ((), ())),
                                    preferred_element_type=jnp.float32)
            sq_t = sqc_ref[0]
            sq_p = sqr_ref[pl.ds(prow, 1), :]
            distance = sq_t + sq_p - 2.0 * inner
            w = jnp.exp(-distance / (scale_factor * width)).astype(jnp.bfloat16)
            num_acc[...] += jnp.dot(w, xp, preferred_element_type=jnp.float32)
            den_acc[...] += jnp.sum(w.astype(jnp.float32), axis=1, keepdims=True)

        for k, p_ref in enumerate(p_refs):
            @pl.when(comp & (src == k))
            def _():
                contribute(p_ref)

        @pl.when(tab[base + C_LAST] == 1)
        def _():
            if mode == "final":
                outs[0][0] = (num_acc[...] / den_acc[...]).astype(outs[0].dtype)
            else:
                num_out = outs[0] if mode != "init" else refs[3 + nsrc]
                den_out = outs[1] if mode != "init" else refs[4 + nsrc]
                num_out[0] = num_acc[...]
                den_out[0] = den_acc[...]

    return kernel


def run_phase(mode, tab, steps, own, sq_col, sources, sq_rows, num=None, den=None):
    nloc, block, width = own.shape
    nsrc = len(sources)
    blk = (1, block, width)
    cblk = (1, block, 1)

    def t_map(i, tab):
        return (tab[i * NCOL + C_T], 0, 0)

    def src_map(k):
        def m(i, tab):
            return (tab[i * NCOL + C_IDX + k], 0, 0)
        return m

    in_specs = ([pl.BlockSpec(blk, t_map), pl.BlockSpec(cblk, t_map)]
                + [pl.BlockSpec(blk, src_map(k)) for k in range(nsrc)]
                + [pl.BlockSpec(memory_space=pltpu.VMEM)])
    args = [tab, own, sq_col, *sources, sq_rows]
    aliases = {}
    if mode != "init":
        in_specs += [pl.BlockSpec(blk, t_map), pl.BlockSpec(cblk, t_map)]
        args += [num, den]
    if mode == "final":
        out_specs = pl.BlockSpec(blk, t_map)
        out_shape = jax.ShapeDtypeStruct((nloc, block, width), jnp.bfloat16)
    else:
        out_specs = [pl.BlockSpec(blk, t_map), pl.BlockSpec(cblk, t_map)]
        out_shape = [jax.ShapeDtypeStruct((nloc, block, width), jnp.float32),
                     jax.ShapeDtypeStruct((nloc, block, 1), jnp.float32)]
        if mode == "accum":
            aliases = {len(args) - 2: 0, len(args) - 1: 1}
    grid_spec = pltpu.PrefetchScalarGridSpec(
        num_scalar_prefetch=1,
        grid=(steps,),
        in_specs=in_specs,
        out_specs=out_specs,
        scratch_shapes=[pltpu.VMEM((block, width), jnp.float32),
                        pltpu.VMEM((block, 1), jnp.float32)],
    )
    flops = steps * 4 * block * block * width
    return pl.pallas_call(
        make_kernel(nsrc, mode),
        grid_spec=grid_spec,
        out_shape=out_shape,
        input_output_aliases=aliases,
        compiler_params=pltpu.CompilerParams(dimension_semantics=("arbitrary",)),
        cost_estimate=pl.CostEstimate(flops=flops, transcendentals=steps * block * block,
                                      bytes_accessed=steps * block * width * 2 * 2),
    )(*args)


def local(embeddings, pair_blocks, pair_count):
    total_rows, width = embeddings.shape
    nloc = total_rows // BLOCK
    slots = pair_blocks.shape[0]
    blocks = embeddings.reshape(nloc, BLOCK, width)
    owners = lax.axis_size("dev")
    first_block = (lax.axis_index("group") * owners + lax.axis_index("dev")) * nloc

    nd = shifted(blocks, "dev", -1)
    pd = shifted(blocks, "dev", 1)
    ng = shifted(blocks, "group", -1)
    pg = shifted(blocks, "group", 1)

    own_sq = squares_of(blocks)
    meta = jnp.concatenate([own_sq.reshape(-1),
                            pair_blocks.reshape(-1).astype(jnp.float32),
                            pair_count.astype(jnp.float32)])
    nsq = nloc * BLOCK
    m_nd = shifted(meta, "dev", -1)
    m_pd = shifted(meta, "dev", 1)
    m_ng = shifted(meta, "group", -1)
    m_pg = shifted(meta, "group", 1)

    def sq_of(m):
        return m[:nsq].reshape(nloc, BLOCK)

    def pairs_of(m):
        return (m[nsq:nsq + 2 * slots].astype(jnp.int32).reshape(slots, 2),
                m[nsq + 2 * slots:].astype(jnp.int32))

    pos = jnp.arange(slots, dtype=jnp.int32)
    used = pos < pair_count[0]
    left = jnp.clip(pair_blocks[:, 0] - first_block, 0, nloc - 1)
    right = pair_blocks[:, 1]
    roff = right - first_block
    r_local = roff < nloc
    r_dev = (roff >= nloc) & (roff < 2 * nloc)
    r_grp = ~r_local & ~r_dev
    ridx_dev = roff - nloc
    ridx_grp = right - first_block - owners * nloc
    zeros = jnp.zeros((slots,), jnp.int32)
    sq_col = own_sq[:, :, None]

    diag = jnp.arange(nloc, dtype=jnp.int32)
    t1 = jnp.concatenate([diag, left, roff])
    i1 = jnp.concatenate([diag, roff, left])
    v1 = jnp.concatenate([jnp.ones((nloc,), bool), used & r_local, used & r_local])
    z1 = jnp.zeros_like(t1)
    tab1, n1 = order_table(t1, z1, i1, v1, v1, nloc, 1)
    num, den = run_phase("init", tab1, n1, blocks, sq_col, [blocks], own_sq)

    def prev_entries(m, prev_first, src):
        pairs, count = pairs_of(m)
        u = pos < count[0]
        r = pairs[:, 1] - first_block
        u = u & (r >= 0) & (r < nloc)
        return r, jnp.full((slots,), src, jnp.int32), pairs[:, 0] - prev_first, u

    pr, ps, pi, pu = prev_entries(m_pd, first_block - nloc, 1)
    t2 = jnp.concatenate([diag, left, pr])
    s2 = jnp.concatenate([jnp.zeros((nloc,), jnp.int32), zeros, ps])
    i2 = jnp.concatenate([diag, ridx_dev, pi])
    c2 = jnp.concatenate([jnp.zeros((nloc,), bool), used & r_dev, pu])
    v2 = jnp.concatenate([jnp.ones((nloc,), bool), used & r_dev, pu])
    tab2, n2 = order_table(t2, s2, i2, c2, v2, nloc, 2)
    sq2 = jnp.concatenate([sq_of(m_nd), sq_of(m_pd)], axis=0)
    num, den = run_phase("accum", tab2, n2, blocks, sq_col, [nd, pd], sq2, num, den)

    gr, gs, gi, gu = prev_entries(m_pg, first_block - owners * nloc, 1)
    t3 = jnp.concatenate([diag, left, gr])
    s3 = jnp.concatenate([jnp.zeros((nloc,), jnp.int32), zeros, gs])
    i3 = jnp.concatenate([diag, ridx_grp, gi])
    c3 = jnp.concatenate([jnp.zeros((nloc,), bool), used & r_grp, gu])
    v3 = jnp.concatenate([jnp.ones((nloc,), bool), used & r_grp, gu])
    tab3, n3 = order_table(t3, s3, i3, c3, v3, nloc, 2)
    sq3 = jnp.concatenate([sq_of(m_ng), sq_of(m_pg)], axis=0)
    smoothed = run_phase("final", tab3, n3, blocks, sq_col, [ng, pg], sq3, num, den)
    return smoothed.reshape(total_rows, width)


def solution(mesh):
    placed = (P(("group", "dev"), None), P(("group", "dev"), None), P(("group", "dev")))
    return jax.shard_map(
        local, mesh=mesh, in_specs=placed, out_specs=P(("group", "dev"), None), check_vma=False
    )
```

```python
import jax
import jax.numpy as jnp
from jax import lax
from jax.experimental import pallas as pl
from jax.experimental.pallas import tpu as pltpu
from jax.sharding import PartitionSpec as P

BLOCK = 256
scale_factor = 0.4
VMEM_LIMIT = 56 * 1024 * 1024


def shifted(shard, axis, by):
    devices = lax.axis_size(axis)
    pairs = [(i, i + by) for i in range(devices) if 0 <= i + by < devices]
    return lax.ppermute(shard, axis, pairs)


def squares_of(blocks):
    return jnp.einsum("bsd,bsd->bs", blocks, blocks, preferred_element_type=jnp.float32)


def pack_table(t, s, ix, v, nloc):
    t = jnp.clip(t, 0, nloc - 1)
    ix = jnp.clip(ix, 0, nloc - 1)
    return jnp.stack([t, s, ix, v.astype(jnp.int32)], axis=0).reshape(-1).astype(jnp.int32)


def make_kernel(nsrc, n, mode):
    def kernel(tab, own_ref, sqc_ref, *refs):
        src_refs = refs[:nsrc]
        sqr_ref = refs[nsrc]
        rest = refs[nsrc + 1:]
        if mode == "init":
            num_ref, den_ref = rest
        elif mode == "accum":
            num_in, den_in, num_ref, den_ref = rest
        else:
            num_in, den_in, out_ref, num_ref, den_ref = rest
        nloc = own_ref.shape[0]
        width = own_ref.shape[2]

        if mode == "accum":
            num_ref[...] = num_in[...]
            den_ref[...] = den_in[...]
        else:
            num_ref[...] = jnp.zeros_like(num_ref)
            den_ref[...] = jnp.zeros_like(den_ref)

        def contribute(t, prow, p_ref, ix):
            xt = own_ref[t]
            xp = p_ref[ix]
            inner = lax.dot_general(xt, xp, (((1,), (1,)), ((), ())),
                                    preferred_element_type=jnp.float32)
            sq_t = sqc_ref[t]
            sq_p = sqr_ref[pl.ds(prow, 1), :]
            distance = sq_t + sq_p - 2.0 * inner
            w = jnp.exp(-distance / (scale_factor * width)).astype(jnp.bfloat16)
            num_ref[t] += jnp.dot(w, xp, preferred_element_type=jnp.float32)
            den_ref[t] += jnp.sum(w.astype(jnp.float32), axis=1, keepdims=True)

        def body(j, carry):
            t = tab[j]
            s = tab[n + j]
            ix = tab[2 * n + j]
            used = tab[3 * n + j] == 1
            for k, p_ref in enumerate(src_refs):
                @pl.when(used & (s == k))
                def _():
                    contribute(t, k * nloc + ix, p_ref, ix)
            return carry

        lax.fori_loop(0, n, body, 0)

        if mode == "final":
            def fin(b, carry):
                out_ref[b] = ((num_in[b] + num_ref[b]) / (den_in[b] + den_ref[b])).astype(
                    out_ref.dtype)
                return carry
            lax.fori_loop(0, nloc, fin, 0)

    return kernel


def run_phase(mode, tab, n, own, sq_col, sources, sq_rows, num=None, den=None):
    nloc, block, width = own.shape
    nsrc = len(sources)
    vm = pl.BlockSpec(memory_space=pltpu.VMEM)
    in_specs = [pl.BlockSpec(memory_space=pltpu.SMEM), vm, vm] + [vm] * nsrc + [vm]
    args = [tab, own, sq_col, *sources, sq_rows]
    acc_shapes = [jax.ShapeDtypeStruct((nloc, block, width), jnp.float32),
                  jax.ShapeDtypeStruct((nloc, block, 1), jnp.float32)]
    scratch = []
    if mode != "init":
        in_specs += [vm, vm]
        args += [num, den]
    if mode == "final":
        out_shape = jax.ShapeDtypeStruct((nloc, block, width), jnp.bfloat16)
        out_specs = vm
        scratch = [pltpu.VMEM((nloc, block, width), jnp.float32),
                   pltpu.VMEM((nloc, block, 1), jnp.float32)]
    else:
        out_shape = acc_shapes
        out_specs = [vm, vm]
    flops = n * 4 * block * block * width
    return pl.pallas_call(
        make_kernel(nsrc, n, mode),
        in_specs=in_specs,
        out_specs=out_specs,
        out_shape=out_shape,
        scratch_shapes=scratch,
        compiler_params=pltpu.CompilerParams(vmem_limit_bytes=VMEM_LIMIT),
        cost_estimate=pl.CostEstimate(flops=flops, transcendentals=n * block * block,
                                      bytes_accessed=(nsrc + 3) * nloc * block * width * 2),
    )(*args)


def local(embeddings, pair_blocks, pair_count):
    total_rows, width = embeddings.shape
    nloc = total_rows // BLOCK
    slots = pair_blocks.shape[0]
    blocks = embeddings.reshape(nloc, BLOCK, width)
    owners = lax.axis_size("dev")
    first_block = (lax.axis_index("group") * owners + lax.axis_index("dev")) * nloc

    own_sq = squares_of(blocks)
    meta = jnp.concatenate([own_sq.reshape(-1),
                            pair_blocks.reshape(-1).astype(jnp.float32),
                            pair_count.astype(jnp.float32)])
    nsq = nloc * BLOCK
    m_nd = shifted(meta, "dev", -1)
    m_pd = shifted(meta, "dev", 1)
    m_ng = shifted(meta, "group", -1)
    m_pg = shifted(meta, "group", 1)
    blocks_after, m_nd, m_pd, m_ng, m_pg = lax.optimization_barrier(
        (blocks, m_nd, m_pd, m_ng, m_pg))

    nd = shifted(blocks_after, "dev", -1)
    pd = shifted(blocks_after, "dev", 1)
    ng = shifted(blocks_after, "group", -1)
    pg = shifted(blocks_after, "group", 1)

    def sq_of(m):
        return m[:nsq].reshape(nloc, BLOCK)

    def pairs_of(m):
        return (m[nsq:nsq + 2 * slots].astype(jnp.int32).reshape(slots, 2),
                m[nsq + 2 * slots:].astype(jnp.int32))

    pos = jnp.arange(slots, dtype=jnp.int32)
    used = pos < pair_count[0]
    left = pair_blocks[:, 0] - first_block
    right = pair_blocks[:, 1]
    roff = right - first_block
    r_local = roff < nloc
    r_dev = (roff >= nloc) & (roff < 2 * nloc)
    r_grp = ~r_local & ~r_dev
    ridx_dev = roff - nloc
    ridx_grp = right - first_block - owners * nloc
    zeros = jnp.zeros((slots,), jnp.int32)
    ones = jnp.ones((slots,), jnp.int32)
    sq_col = own_sq[:, :, None]

    diag = jnp.arange(nloc, dtype=jnp.int32)
    t1 = jnp.concatenate([diag, left, roff])
    i1 = jnp.concatenate([diag, roff, left])
    v1 = jnp.concatenate([jnp.ones((nloc,), bool), used & r_local, used & r_local])
    tab1 = pack_table(t1, jnp.zeros_like(t1), i1, v1, nloc)
    num, den = run_phase("init", tab1, t1.shape[0], blocks, sq_col, [blocks], own_sq)

    def prev_entries(m, prev_first):
        pairs, count = pairs_of(m)
        u = pos < count[0]
        r = pairs[:, 1] - first_block
        u = u & (r >= 0) & (r < nloc)
        return r, pairs[:, 0] - prev_first, u

    pr, pi, pu = prev_entries(m_pd, first_block - nloc)
    t2 = jnp.concatenate([left, pr])
    s2 = jnp.concatenate([zeros, ones])
    i2 = jnp.concatenate([ridx_dev, pi])
    v2 = jnp.concatenate([used & r_dev, pu])
    tab2 = pack_table(t2, s2, i2, v2, nloc)
    sq2 = jnp.concatenate([sq_of(m_nd), sq_of(m_pd)], axis=0)
    num, den = run_phase("accum", tab2, t2.shape[0], blocks, sq_col, [nd, pd], sq2, num, den)

    gr, gi, gu = prev_entries(m_pg, first_block - owners * nloc)
    t3 = jnp.concatenate([left, gr])
    s3 = jnp.concatenate([zeros, ones])
    i3 = jnp.concatenate([ridx_grp, gi])
    v3 = jnp.concatenate([used & r_grp, gu])
    tab3 = pack_table(t3, s3, i3, v3, nloc)
    sq3 = jnp.concatenate([sq_of(m_ng), sq_of(m_pg)], axis=0)
    smoothed = run_phase("final", tab3, t3.shape[0], blocks, sq_col, [ng, pg], sq3, num, den)
    return smoothed.reshape(total_rows, width)


def solution(mesh):
    placed = (P(("group", "dev"), None), P(("group", "dev"), None), P(("group", "dev")))
    return jax.shard_map(
        local, mesh=mesh, in_specs=placed, out_specs=P(("group", "dev"), None), check_vma=False
    )
```

```python
import jax
import jax.numpy as jnp
from jax import lax
from jax.experimental import pallas as pl
from jax.experimental.pallas import tpu as pltpu
from jax.sharding import PartitionSpec as P

BLOCK = 256
scale_factor = 0.4
VMEM_LIMIT = 56 * 1024 * 1024


def shifted(shard, axis, by):
    devices = lax.axis_size(axis)
    pairs = [(i, i + by) for i in range(devices) if 0 <= i + by < devices]
    return lax.ppermute(shard, axis, pairs)


def squares_of(blocks):
    return jnp.einsum("bsd,bsd->bs", blocks, blocks, preferred_element_type=jnp.float32)


def pack_table(t, s, ix, v, nloc):
    t = jnp.clip(t, 0, nloc - 1)
    ix = jnp.clip(ix, 0, nloc - 1)
    return jnp.stack([t, s, ix, v.astype(jnp.int32)], axis=0).reshape(-1).astype(jnp.int32)


def make_kernel(nsrc, n, mode):
    def kernel(tab, own_ref, sqc_ref, *refs):
        src_refs = refs[:nsrc]
        sqr_ref = refs[nsrc]
        rest = refs[nsrc + 1:]
        if mode == "init":
            num_ref, den_ref = rest
        elif mode == "accum":
            num_in, den_in, num_ref, den_ref = rest
        else:
            num_in, den_in, out_ref, num_ref, den_ref = rest
        nloc = own_ref.shape[0] // BLOCK
        width = own_ref.shape[1]

        if mode == "accum":
            num_ref[...] = num_in[...]
            den_ref[...] = den_in[...]
        else:
            num_ref[...] = jnp.zeros_like(num_ref)
            den_ref[...] = jnp.zeros_like(den_ref)

        def contribute(t, prow, p_ref, ix):
            xt = own_ref[pl.ds(pl.multiple_of(t * BLOCK, BLOCK), BLOCK), :]
            xp = p_ref[pl.ds(pl.multiple_of(ix * BLOCK, BLOCK), BLOCK), :]
            inner = lax.dot_general(xt, xp, (((1,), (1,)), ((), ())),
                                    preferred_element_type=jnp.float32)
            sq_t = sqc_ref[t]
            sq_p = sqr_ref[pl.ds(prow, 1), :]
            distance = sq_t + sq_p - 2.0 * inner
            w = jnp.exp(-distance / (scale_factor * width)).astype(jnp.bfloat16)
            num_ref[t] += jnp.dot(w, xp, preferred_element_type=jnp.float32)
            den_ref[t] += jnp.sum(w.astype(jnp.float32), axis=1, keepdims=True)

        def body(j, carry):
            t = tab[j]
            s = tab[n + j]
            ix = tab[2 * n + j]
            used = tab[3 * n + j] == 1
            for k, p_ref in enumerate(src_refs):
                @pl.when(used & (s == k))
                def _():
                    contribute(t, k * nloc + ix, p_ref, ix)
            return carry

        lax.fori_loop(0, n, body, 0)

        if mode == "final":
            def fin(b, carry):
                out_ref[b] = ((num_in[b] + num_ref[b]) / (den_in[b] + den_ref[b])).astype(
                    out_ref.dtype)
                return carry
            lax.fori_loop(0, nloc, fin, 0)

    return kernel


def run_phase(mode, tab, n, own, sq_col, sources, sq_rows, num=None, den=None):
    rows, width = own.shape
    block = BLOCK
    nloc = rows // block
    nsrc = len(sources)
    vm = pl.BlockSpec(memory_space=pltpu.VMEM)
    in_specs = [pl.BlockSpec(memory_space=pltpu.SMEM), vm, vm] + [vm] * nsrc + [vm]
    args = [tab, own, sq_col, *sources, sq_rows]
    acc_shapes = [jax.ShapeDtypeStruct((nloc, block, width), jnp.float32),
                  jax.ShapeDtypeStruct((nloc, block, 1), jnp.float32)]
    scratch = []
    if mode != "init":
        in_specs += [vm, vm]
        args += [num, den]
    if mode == "final":
        out_shape = jax.ShapeDtypeStruct((nloc, block, width), jnp.bfloat16)
        out_specs = vm
        scratch = [pltpu.VMEM((nloc, block, width), jnp.float32),
                   pltpu.VMEM((nloc, block, 1), jnp.float32)]
    else:
        out_shape = acc_shapes
        out_specs = [vm, vm]
    flops = n * 4 * block * block * width
    return pl.pallas_call(
        make_kernel(nsrc, n, mode),
        in_specs=in_specs,
        out_specs=out_specs,
        out_shape=out_shape,
        scratch_shapes=scratch,
        compiler_params=pltpu.CompilerParams(vmem_limit_bytes=VMEM_LIMIT),
        cost_estimate=pl.CostEstimate(flops=flops, transcendentals=n * block * block,
                                      bytes_accessed=(nsrc + 3) * nloc * block * width * 2),
    )(*args)


def encode_meta(own_sq, pair_blocks, pair_count, width):
    nloc = own_sq.shape[0]
    hi = lax.reduce_precision(own_sq, exponent_bits=8, mantissa_bits=7)
    r1 = own_sq - hi
    mid = lax.reduce_precision(r1, exponent_bits=8, mantissa_bits=7)
    lo = r1 - mid
    pieces = jnp.concatenate([hi, mid, lo], axis=0)
    pieces = jnp.pad(pieces, ((0, 0), (0, width - pieces.shape[1])))
    ids = pair_blocks.reshape(1, -1) + 1
    ints = jnp.concatenate([ids // 64, ids % 64], axis=0)
    ints = jnp.pad(ints, ((0, 0), (0, width - ints.shape[1])))
    cnt = jnp.pad(pair_count.reshape(1, 1), ((0, 0), (0, width - 1)))
    meta = jnp.concatenate([pieces, ints.astype(jnp.float32), cnt.astype(jnp.float32)], axis=0)
    pad_rows = -meta.shape[0] % 16
    meta = jnp.pad(meta, ((0, pad_rows), (0, 0)))
    return meta.astype(jnp.bfloat16)


def decode_meta(recv, nloc, slots):
    meta = recv[nloc * BLOCK:].astype(jnp.float32)
    sq = (meta[:nloc, :BLOCK] + meta[nloc:2 * nloc, :BLOCK]) + meta[2 * nloc:3 * nloc, :BLOCK]
    ids = meta[3 * nloc, :2 * slots] * 64.0 + meta[3 * nloc + 1, :2 * slots]
    pairs = ids.astype(jnp.int32).reshape(slots, 2) - 1
    count = meta[3 * nloc + 2, :1].astype(jnp.int32)
    return sq, pairs, count


def local(embeddings, pair_blocks, pair_count):
    total_rows, width = embeddings.shape
    nloc = total_rows // BLOCK
    slots = pair_blocks.shape[0]
    blocks = embeddings.reshape(nloc, BLOCK, width)
    owners = lax.axis_size("dev")
    first_block = (lax.axis_index("group") * owners + lax.axis_index("dev")) * nloc

    own_sq = squares_of(blocks)
    payload = jnp.concatenate(
        [embeddings, encode_meta(own_sq, pair_blocks, pair_count, width)], axis=0)
    nd = shifted(payload, "dev", -1)
    pd = shifted(payload, "dev", 1)
    ng = shifted(payload, "group", -1)
    pg = shifted(payload, "group", 1)

    pos = jnp.arange(slots, dtype=jnp.int32)
    used = pos < pair_count[0]
    left = pair_blocks[:, 0] - first_block
    right = pair_blocks[:, 1]
    roff = right - first_block
    r_local = roff < nloc
    r_dev = (roff >= nloc) & (roff < 2 * nloc)
    r_grp = ~r_local & ~r_dev
    ridx_dev = roff - nloc
    ridx_grp = right - first_block - owners * nloc
    zeros = jnp.zeros((slots,), jnp.int32)
    ones = jnp.ones((slots,), jnp.int32)
    sq_col = own_sq[:, :, None]

    diag = jnp.arange(nloc, dtype=jnp.int32)
    t1 = jnp.concatenate([diag, left, roff])
    i1 = jnp.concatenate([diag, roff, left])
    v1 = jnp.concatenate([jnp.ones((nloc,), bool), used & r_local, used & r_local])
    tab1 = pack_table(t1, jnp.zeros_like(t1), i1, v1, nloc)
    num, den = run_phase("init", tab1, t1.shape[0], embeddings, sq_col, [embeddings], own_sq)

    def prev_entries(pairs, count, prev_first):
        u = pos < count[0]
        r = pairs[:, 1] - first_block
        u = u & (r >= 0) & (r < nloc)
        return r, pairs[:, 0] - prev_first, u

    nd, pd, num, den = lax.optimization_barrier((nd, pd, num, den))
    sq_nd, _, _ = decode_meta(nd, nloc, slots)
    sq_pd, pd_pairs, pd_count = decode_meta(pd, nloc, slots)
    pr, pi, pu = prev_entries(pd_pairs, pd_count, first_block - nloc)
    t2 = jnp.concatenate([left, pr])
    s2 = jnp.concatenate([zeros, ones])
    i2 = jnp.concatenate([ridx_dev, pi])
    v2 = jnp.concatenate([used & r_dev, pu])
    tab2 = pack_table(t2, s2, i2, v2, nloc)
    sq2 = jnp.concatenate([sq_nd, sq_pd], axis=0)
    num, den = run_phase("accum", tab2, t2.shape[0], embeddings, sq_col, [nd, pd], sq2, num, den)

    ng, pg, num, den = lax.optimization_barrier((ng, pg, num, den))
    sq_ng, _, _ = decode_meta(ng, nloc, slots)
    sq_pg, pg_pairs, pg_count = decode_meta(pg, nloc, slots)
    gr, gi, gu = prev_entries(pg_pairs, pg_count, first_block - owners * nloc)
    t3 = jnp.concatenate([left, gr])
    s3 = jnp.concatenate([zeros, ones])
    i3 = jnp.concatenate([ridx_grp, gi])
    v3 = jnp.concatenate([used & r_grp, gu])
    tab3 = pack_table(t3, s3, i3, v3, nloc)
    sq3 = jnp.concatenate([sq_ng, sq_pg], axis=0)
    smoothed = run_phase("final", tab3, t3.shape[0], embeddings, sq_col, [ng, pg], sq3, num, den)
    return smoothed.reshape(total_rows, width)


def solution(mesh):
    placed = (P(("group", "dev"), None), P(("group", "dev"), None), P(("group", "dev")))
    return jax.shard_map(
        local, mesh=mesh, in_specs=placed, out_specs=P(("group", "dev"), None), check_vma=False
    )
```

```python
import functools

import jax
import jax.numpy as jnp
from jax import lax
from jax.experimental import pallas as pl
from jax.experimental.pallas import tpu as pltpu
from jax.sharding import PartitionSpec as P

BLOCK = 256
scale_factor = 0.4
VMEM_LIMIT = 56 * 1024 * 1024


def shifted(shard, axis, by):
    devices = lax.axis_size(axis)
    pairs = [(i, i + by) for i in range(devices) if 0 <= i + by < devices]
    return lax.ppermute(shard, axis, pairs)


def squares_of(blocks):
    return jnp.einsum("bsd,bsd->bs", blocks, blocks, preferred_element_type=jnp.float32)


def pack_table(t, s, ix, v, nloc):
    t = jnp.clip(t, 0, nloc - 1)
    ix = jnp.clip(ix, 0, nloc - 1)
    return jnp.stack([t, s, ix, v.astype(jnp.int32)], axis=0).reshape(-1).astype(jnp.int32)


def make_kernel(nsrc, n, mode):
    def kernel(tab, own_ref, sqc_ref, *refs):
        src_refs = refs[:nsrc]
        sqr_ref = refs[nsrc]
        rest = refs[nsrc + 1:]
        if mode == "init":
            num_ref, den_ref = rest
        elif mode == "accum":
            num_in, den_in, num_ref, den_ref = rest
        else:
            num_in, den_in, out_ref, num_ref, den_ref = rest
        nloc = own_ref.shape[0] // BLOCK
        width = own_ref.shape[1]

        if mode == "accum":
            num_ref[...] = num_in[...]
            den_ref[...] = den_in[...]
        else:
            num_ref[...] = jnp.zeros_like(num_ref)
            den_ref[...] = jnp.zeros_like(den_ref)

        def contribute(t, prow, p_ref, ix):
            xt = own_ref[pl.ds(pl.multiple_of(t * BLOCK, BLOCK), BLOCK), :]
            xp = p_ref[pl.ds(pl.multiple_of(ix * BLOCK, BLOCK), BLOCK), :]
            inner = lax.dot_general(xt, xp, (((1,), (1,)), ((), ())),
                                    preferred_element_type=jnp.float32)
            sq_t = sqc_ref[t]
            sq_p = sqr_ref[pl.ds(prow, 1), :]
            distance = sq_t + sq_p - 2.0 * inner
            w = jnp.exp(-distance / (scale_factor * width)).astype(jnp.bfloat16)
            num_ref[t] += jnp.dot(w, xp, preferred_element_type=jnp.float32)
            den_ref[t] += jnp.sum(w.astype(jnp.float32), axis=1, keepdims=True)

        def body(j, carry):
            t = tab[j]
            s = tab[n + j]
            ix = tab[2 * n + j]
            used = tab[3 * n + j] == 1
            for k, p_ref in enumerate(src_refs):
                @pl.when(used & (s == k))
                def _():
                    contribute(t, k * nloc + ix, p_ref, ix)
            return carry

        lax.fori_loop(0, n, body, 0)

        if mode == "final":
            def fin(b, carry):
                out_ref[b] = ((num_in[b] + num_ref[b]) / (den_in[b] + den_ref[b])).astype(
                    out_ref.dtype)
                return carry
            lax.fori_loop(0, nloc, fin, 0)

    return kernel


def run_phase(mode, tab, n, own, sq_col, sources, sq_rows, num=None, den=None):
    rows, width = own.shape
    block = BLOCK
    nloc = rows // block
    nsrc = len(sources)
    vm = pl.BlockSpec(memory_space=pltpu.VMEM)
    in_specs = [pl.BlockSpec(memory_space=pltpu.SMEM), vm, vm] + [vm] * nsrc + [vm]
    args = [tab, own, sq_col, *sources, sq_rows]
    acc_shapes = [jax.ShapeDtypeStruct((nloc, block, width), jnp.float32),
                  jax.ShapeDtypeStruct((nloc, block, 1), jnp.float32)]
    scratch = []
    if mode != "init":
        in_specs += [vm, vm]
        args += [num, den]
    if mode == "final":
        out_shape = jax.ShapeDtypeStruct((nloc, block, width), jnp.bfloat16)
        out_specs = vm
        scratch = [pltpu.VMEM((nloc, block, width), jnp.float32),
                   pltpu.VMEM((nloc, block, 1), jnp.float32)]
    else:
        out_shape = acc_shapes
        out_specs = [vm, vm]
    flops = n * 4 * block * block * width
    return pl.pallas_call(
        make_kernel(nsrc, n, mode),
        in_specs=in_specs,
        out_specs=out_specs,
        out_shape=out_shape,
        scratch_shapes=scratch,
        compiler_params=pltpu.CompilerParams(vmem_limit_bytes=VMEM_LIMIT),
        cost_estimate=pl.CostEstimate(flops=flops, transcendentals=n * block * block,
                                      bytes_accessed=(nsrc + 3) * nloc * block * width * 2),
    )(*args)


def final_kernel(n, tab, own_ref, sqc_ref, sqr_ref, num_ref, den_ref, src0, src1,
                 out_ref, xp_buf, sem, acc, dacc):
    b = pl.program_id(0)
    nloc = sqr_ref.shape[0] // 2
    width = own_ref.shape[1]
    acc[...] = num_ref[0]
    dacc[...] = den_ref[0]

    def body(j, carry):
        t = tab[j]
        s = tab[n + j]
        ix = tab[2 * n + j]
        hit = (tab[3 * n + j] == 1) & (t == b)
        rows = pl.ds(pl.multiple_of(ix * BLOCK, BLOCK), BLOCK)

        for k, src in enumerate((src0, src1)):
            @pl.when(hit & (s == k))
            def _():
                cp = pltpu.make_async_copy(src.at[rows], xp_buf, sem.at[0])
                cp.start()
                cp.wait()

        @pl.when(hit)
        def _():
            xt = own_ref[...]
            xp = xp_buf[...]
            inner = lax.dot_general(xt, xp, (((1,), (1,)), ((), ())),
                                    preferred_element_type=jnp.float32)
            sq_p = sqr_ref[pl.ds(s * nloc + ix, 1), :]
            distance = sqc_ref[0] + sq_p - 2.0 * inner
            w = jnp.exp(-distance / (scale_factor * width)).astype(jnp.bfloat16)
            acc[...] += jnp.dot(w, xp, preferred_element_type=jnp.float32)
            dacc[...] += jnp.sum(w.astype(jnp.float32), axis=1, keepdims=True)
        return carry

    lax.fori_loop(0, n, body, 0)
    out_ref[0] = (acc[...] / dacc[...]).astype(out_ref.dtype)


def run_final(tab, n, own, sq_col, sources, sq_rows, num, den):
    rows, width = own.shape
    nloc = rows // BLOCK
    blk = (1, BLOCK, width)
    cblk = (1, BLOCK, 1)
    grid_spec = pltpu.PrefetchScalarGridSpec(
        num_scalar_prefetch=1,
        grid=(nloc,),
        in_specs=[pl.BlockSpec((BLOCK, width), lambda b, tab: (b, 0)),
                  pl.BlockSpec(cblk, lambda b, tab: (b, 0, 0)),
                  pl.BlockSpec(memory_space=pltpu.VMEM),
                  pl.BlockSpec(blk, lambda b, tab: (b, 0, 0)),
                  pl.BlockSpec(cblk, lambda b, tab: (b, 0, 0)),
                  pl.BlockSpec(memory_space=pl.ANY),
                  pl.BlockSpec(memory_space=pl.ANY)],
        out_specs=pl.BlockSpec(blk, lambda b, tab: (b, 0, 0)),
        scratch_shapes=[pltpu.VMEM((BLOCK, width), jnp.bfloat16),
                        pltpu.SemaphoreType.DMA((1,)),
                        pltpu.VMEM((BLOCK, width), jnp.float32),
                        pltpu.VMEM((BLOCK, 1), jnp.float32)],
    )
    flops = n * 4 * BLOCK * BLOCK * width
    return pl.pallas_call(
        functools.partial(final_kernel, n),
        grid_spec=grid_spec,
        out_shape=jax.ShapeDtypeStruct((nloc, BLOCK, width), jnp.bfloat16),
        compiler_params=pltpu.CompilerParams(dimension_semantics=("arbitrary",)),
        cost_estimate=pl.CostEstimate(flops=flops, transcendentals=n * BLOCK * BLOCK,
                                      bytes_accessed=nloc * BLOCK * width * 8),
    )(tab, own, sq_col, sq_rows, num, den, *sources)


def encode_meta(own_sq, pair_blocks, pair_count, width):
    nloc = own_sq.shape[0]
    hi = lax.reduce_precision(own_sq, exponent_bits=8, mantissa_bits=7)
    r1 = own_sq - hi
    mid = lax.reduce_precision(r1, exponent_bits=8, mantissa_bits=7)
    lo = r1 - mid
    pieces = jnp.concatenate([hi, mid, lo], axis=0)
    pieces = jnp.pad(pieces, ((0, 0), (0, width - pieces.shape[1])))
    ids = pair_blocks.reshape(1, -1) + 1
    ints = jnp.concatenate([ids // 64, ids % 64], axis=0)
    ints = jnp.pad(ints, ((0, 0), (0, width - ints.shape[1])))
    cnt = jnp.pad(pair_count.reshape(1, 1), ((0, 0), (0, width - 1)))
    meta = jnp.concatenate([pieces, ints.astype(jnp.float32), cnt.astype(jnp.float32)], axis=0)
    pad_rows = -meta.shape[0] % 16
    meta = jnp.pad(meta, ((0, pad_rows), (0, 0)))
    return meta.astype(jnp.bfloat16)


def decode_meta(recv, nloc, slots):
    meta = recv[nloc * BLOCK:].astype(jnp.float32)
    sq = (meta[:nloc, :BLOCK] + meta[nloc:2 * nloc, :BLOCK]) + meta[2 * nloc:3 * nloc, :BLOCK]
    ids = meta[3 * nloc, :2 * slots] * 64.0 + meta[3 * nloc + 1, :2 * slots]
    pairs = ids.astype(jnp.int32).reshape(slots, 2) - 1
    count = meta[3 * nloc + 2, :1].astype(jnp.int32)
    return sq, pairs, count


def local(embeddings, pair_blocks, pair_count):
    total_rows, width = embeddings.shape
    nloc = total_rows // BLOCK
    slots = pair_blocks.shape[0]
    blocks = embeddings.reshape(nloc, BLOCK, width)
    owners = lax.axis_size("dev")
    first_block = (lax.axis_index("group") * owners + lax.axis_index("dev")) * nloc

    own_sq = squares_of(blocks)
    payload = jnp.concatenate(
        [embeddings, encode_meta(own_sq, pair_blocks, pair_count, width)], axis=0)
    nd = shifted(payload, "dev", -1)
    pd = shifted(payload, "dev", 1)
    ng = shifted(payload, "group", -1)
    pg = shifted(payload, "group", 1)

    pos = jnp.arange(slots, dtype=jnp.int32)
    used = pos < pair_count[0]
    left = pair_blocks[:, 0] - first_block
    right = pair_blocks[:, 1]
    roff = right - first_block
    r_local = roff < nloc
    r_dev = (roff >= nloc) & (roff < 2 * nloc)
    r_grp = ~r_local & ~r_dev
    ridx_dev = roff - nloc
    ridx_grp = right - first_block - owners * nloc
    zeros = jnp.zeros((slots,), jnp.int32)
    ones = jnp.ones((slots,), jnp.int32)
    sq_col = own_sq[:, :, None]

    diag = jnp.arange(nloc, dtype=jnp.int32)
    t1 = jnp.concatenate([diag, left, roff])
    i1 = jnp.concatenate([diag, roff, left])
    v1 = jnp.concatenate([jnp.ones((nloc,), bool), used & r_local, used & r_local])
    tab1 = pack_table(t1, jnp.zeros_like(t1), i1, v1, nloc)
    num, den = run_phase("init", tab1, t1.shape[0], embeddings, sq_col, [embeddings], own_sq)

    def prev_entries(pairs, count, prev_first):
        u = pos < count[0]
        r = pairs[:, 1] - first_block
        u = u & (r >= 0) & (r < nloc)
        return r, pairs[:, 0] - prev_first, u

    nd, pd, num, den = lax.optimization_barrier((nd, pd, num, den))
    sq_nd, _, _ = decode_meta(nd, nloc, slots)
    sq_pd, pd_pairs, pd_count = decode_meta(pd, nloc, slots)
    pr, pi, pu = prev_entries(pd_pairs, pd_count, first_block - nloc)
    t2 = jnp.concatenate([left, pr])
    s2 = jnp.concatenate([zeros, ones])
    i2 = jnp.concatenate([ridx_dev, pi])
    v2 = jnp.concatenate([used & r_dev, pu])
    tab2 = pack_table(t2, s2, i2, v2, nloc)
    sq2 = jnp.concatenate([sq_nd, sq_pd], axis=0)
    num, den = run_phase("accum", tab2, t2.shape[0], embeddings, sq_col, [nd, pd], sq2, num, den)

    ng, pg, num, den = lax.optimization_barrier((ng, pg, num, den))
    sq_ng, _, _ = decode_meta(ng, nloc, slots)
    sq_pg, pg_pairs, pg_count = decode_meta(pg, nloc, slots)
    gr, gi, gu = prev_entries(pg_pairs, pg_count, first_block - owners * nloc)
    t3 = jnp.concatenate([left, gr])
    s3 = jnp.concatenate([zeros, ones])
    i3 = jnp.concatenate([ridx_grp, gi])
    v3 = jnp.concatenate([used & r_grp, gu])
    tab3 = pack_table(t3, s3, i3, v3, nloc)
    sq3 = jnp.concatenate([sq_ng, sq_pg], axis=0)
    smoothed = run_final(tab3, t3.shape[0], embeddings, sq_col, [ng, pg], sq3, num, den)
    return smoothed.reshape(total_rows, width)


def solution(mesh):
    placed = (P(("group", "dev"), None), P(("group", "dev"), None), P(("group", "dev")))
    return jax.shard_map(
        local, mesh=mesh, in_specs=placed, out_specs=P(("group", "dev"), None), check_vma=False
    )
```

```python
import jax
import jax.numpy as jnp
from jax import lax
from jax.experimental import pallas as pl
from jax.experimental.pallas import tpu as pltpu
from jax.sharding import PartitionSpec as P

BLOCK = 256
scale_factor = 0.4
VMEM_LIMIT = 56 * 1024 * 1024


def shifted(shard, axis, by):
    devices = lax.axis_size(axis)
    pairs = [(i, i + by) for i in range(devices) if 0 <= i + by < devices]
    return lax.ppermute(shard, axis, pairs)


def squares_of(blocks):
    return jnp.einsum("bsd,bsd->bs", blocks, blocks, preferred_element_type=jnp.float32)


def pack_table(t, s, ix, v, nloc):
    t = jnp.clip(t, 0, nloc - 1)
    ix = jnp.clip(ix, 0, nloc - 1)
    return jnp.stack([t, s, ix, v.astype(jnp.int32)], axis=0).reshape(-1).astype(jnp.int32)


def make_kernel(nsrc, n, mode):
    def kernel(tab, own_ref, sqc_ref, *refs):
        src_refs = refs[:nsrc]
        sqr_ref = refs[nsrc]
        rest = refs[nsrc + 1:]
        if mode == "init":
            num_ref, den_ref = rest
        elif mode == "accum":
            num_in, den_in, num_ref, den_ref = rest
        else:
            num_in, den_in, out_ref, num_ref, den_ref, xp_buf, sem = rest
        nloc = own_ref.shape[0] // BLOCK
        width = own_ref.shape[1]

        if mode != "init":
            num_ref[...] = num_in[...]
            den_ref[...] = den_in[...]
        else:
            num_ref[...] = jnp.zeros_like(num_ref)
            den_ref[...] = jnp.zeros_like(den_ref)

        def contribute(t, prow, p_ref, ix):
            xt = own_ref[pl.ds(pl.multiple_of(t * BLOCK, BLOCK), BLOCK), :]
            xp = p_ref[pl.ds(pl.multiple_of(ix * BLOCK, BLOCK), BLOCK), :]
            inner = lax.dot_general(xt, xp, (((1,), (1,)), ((), ())),
                                    preferred_element_type=jnp.float32)
            sq_t = sqc_ref[t]
            sq_p = sqr_ref[pl.ds(prow, 1), :]
            distance = sq_t + sq_p - 2.0 * inner
            w = jnp.exp(-distance / (scale_factor * width)).astype(jnp.bfloat16)
            num_ref[t] += jnp.dot(w, xp, preferred_element_type=jnp.float32)
            den_ref[t] += jnp.sum(w.astype(jnp.float32), axis=1, keepdims=True)

        def body(j, carry):
            t = tab[j]
            s = tab[n + j]
            ix = tab[2 * n + j]
            used = tab[3 * n + j] == 1
            if mode == "final":
                for k, p_ref in enumerate(src_refs):
                    @pl.when(used & (s == k))
                    def _():
                        rows = pl.ds(pl.multiple_of(ix * BLOCK, BLOCK), BLOCK)
                        cp = pltpu.make_async_copy(p_ref.at[rows], xp_buf, sem.at[0])
                        cp.start()
                        cp.wait()

                @pl.when(used)
                def _():
                    contribute(t, s * nloc + ix, xp_buf, 0)
            else:
                for k, p_ref in enumerate(src_refs):
                    @pl.when(used & (s == k))
                    def _():
                        contribute(t, k * nloc + ix, p_ref, ix)
            return carry

        lax.fori_loop(0, n, body, 0)

        if mode == "final":
            def fin(b, carry):
                out_ref[b] = (num_ref[b] / den_ref[b]).astype(out_ref.dtype)
                return carry
            lax.fori_loop(0, nloc, fin, 0)

    return kernel


def run_phase(mode, tab, n, own, sq_col, sources, sq_rows, num=None, den=None):
    rows, width = own.shape
    block = BLOCK
    nloc = rows // block
    nsrc = len(sources)
    vm = pl.BlockSpec(memory_space=pltpu.VMEM)
    src_space = pl.BlockSpec(memory_space=pl.ANY) if mode == "final" else vm
    in_specs = [pl.BlockSpec(memory_space=pltpu.SMEM), vm, vm] + [src_space] * nsrc + [vm]
    args = [tab, own, sq_col, *sources, sq_rows]
    acc_shapes = [jax.ShapeDtypeStruct((nloc, block, width), jnp.float32),
                  jax.ShapeDtypeStruct((nloc, block, 1), jnp.float32)]
    scratch = []
    if mode != "init":
        in_specs += [vm, vm]
        args += [num, den]
    if mode == "final":
        out_shape = jax.ShapeDtypeStruct((nloc, block, width), jnp.bfloat16)
        out_specs = vm
        scratch = [pltpu.VMEM((nloc, block, width), jnp.float32),
                   pltpu.VMEM((nloc, block, 1), jnp.float32),
                   pltpu.VMEM((block, width), jnp.bfloat16),
                   pltpu.SemaphoreType.DMA((1,))]
    else:
        out_shape = acc_shapes
        out_specs = [vm, vm]
    flops = n * 4 * block * block * width
    return pl.pallas_call(
        make_kernel(nsrc, n, mode),
        in_specs=in_specs,
        out_specs=out_specs,
        out_shape=out_shape,
        scratch_shapes=scratch,
        compiler_params=pltpu.CompilerParams(vmem_limit_bytes=VMEM_LIMIT),
        cost_estimate=pl.CostEstimate(flops=flops, transcendentals=n * block * block,
                                      bytes_accessed=(nsrc + 3) * nloc * block * width * 2),
    )(*args)


def encode_meta(own_sq, pair_blocks, pair_count, width):
    nloc = own_sq.shape[0]
    hi = lax.reduce_precision(own_sq, exponent_bits=8, mantissa_bits=7)
    r1 = own_sq - hi
    mid = lax.reduce_precision(r1, exponent_bits=8, mantissa_bits=7)
    lo = r1 - mid
    pieces = jnp.concatenate([hi, mid, lo], axis=0)
    pieces = jnp.pad(pieces, ((0, 0), (0, width - pieces.shape[1])))
    ids = pair_blocks.reshape(1, -1) + 1
    ints = jnp.concatenate([ids // 64, ids % 64], axis=0)
    ints = jnp.pad(ints, ((0, 0), (0, width - ints.shape[1])))
    cnt = jnp.pad(pair_count.reshape(1, 1), ((0, 0), (0, width - 1)))
    meta = jnp.concatenate([pieces, ints.astype(jnp.float32), cnt.astype(jnp.float32)], axis=0)
    pad_rows = -meta.shape[0] % 16
    meta = jnp.pad(meta, ((0, pad_rows), (0, 0)))
    return meta.astype(jnp.bfloat16)


def decode_meta(recv, nloc, slots):
    meta = recv[nloc * BLOCK:].astype(jnp.float32)
    sq = (meta[:nloc, :BLOCK] + meta[nloc:2 * nloc, :BLOCK]) + meta[2 * nloc:3 * nloc, :BLOCK]
    ids = meta[3 * nloc, :2 * slots] * 64.0 + meta[3 * nloc + 1, :2 * slots]
    pairs = ids.astype(jnp.int32).reshape(slots, 2) - 1
    count = meta[3 * nloc + 2, :1].astype(jnp.int32)
    return sq, pairs, count


def local(embeddings, pair_blocks, pair_count):
    total_rows, width = embeddings.shape
    nloc = total_rows // BLOCK
    slots = pair_blocks.shape[0]
    blocks = embeddings.reshape(nloc, BLOCK, width)
    owners = lax.axis_size("dev")
    first_block = (lax.axis_index("group") * owners + lax.axis_index("dev")) * nloc

    own_sq = squares_of(blocks)
    payload = jnp.concatenate(
        [embeddings, encode_meta(own_sq, pair_blocks, pair_count, width)], axis=0)
    nd = shifted(payload, "dev", -1)
    pd = shifted(payload, "dev", 1)
    ng = shifted(payload, "group", -1)
    pg = shifted(payload, "group", 1)

    pos = jnp.arange(slots, dtype=jnp.int32)
    used = pos < pair_count[0]
    left = pair_blocks[:, 0] - first_block
    right = pair_blocks[:, 1]
    roff = right - first_block
    r_local = roff < nloc
    r_dev = (roff >= nloc) & (roff < 2 * nloc)
    r_grp = ~r_local & ~r_dev
    ridx_dev = roff - nloc
    ridx_grp = right - first_block - owners * nloc
    zeros = jnp.zeros((slots,), jnp.int32)
    ones = jnp.ones((slots,), jnp.int32)
    sq_col = own_sq[:, :, None]

    diag = jnp.arange(nloc, dtype=jnp.int32)
    t1 = jnp.concatenate([diag, left, roff])
    i1 = jnp.concatenate([diag, roff, left])
    v1 = jnp.concatenate([jnp.ones((nloc,), bool), used & r_local, used & r_local])
    tab1 = pack_table(t1, jnp.zeros_like(t1), i1, v1, nloc)
    num, den = run_phase("init", tab1, t1.shape[0], embeddings, sq_col, [embeddings], own_sq)

    def prev_entries(pairs, count, prev_first):
        u = pos < count[0]
        r = pairs[:, 1] - first_block
        u = u & (r >= 0) & (r < nloc)
        return r, pairs[:, 0] - prev_first, u

    nd, pd, num, den = lax.optimization_barrier((nd, pd, num, den))
    sq_nd, _, _ = decode_meta(nd, nloc, slots)
    sq_pd, pd_pairs, pd_count = decode_meta(pd, nloc, slots)
    pr, pi, pu = prev_entries(pd_pairs, pd_count, first_block - nloc)
    t2 = jnp.concatenate([left, pr])
    s2 = jnp.concatenate([zeros, ones])
    i2 = jnp.concatenate([ridx_dev, pi])
    v2 = jnp.concatenate([used & r_dev, pu])
    tab2 = pack_table(t2, s2, i2, v2, nloc)
    sq2 = jnp.concatenate([sq_nd, sq_pd], axis=0)
    num, den = run_phase("accum", tab2, t2.shape[0], embeddings, sq_col, [nd, pd], sq2, num, den)

    ng, pg, num, den = lax.optimization_barrier((ng, pg, num, den))
    sq_ng, _, _ = decode_meta(ng, nloc, slots)
    sq_pg, pg_pairs, pg_count = decode_meta(pg, nloc, slots)
    gr, gi, gu = prev_entries(pg_pairs, pg_count, first_block - owners * nloc)
    t3 = jnp.concatenate([left, gr])
    s3 = jnp.concatenate([zeros, ones])
    i3 = jnp.concatenate([ridx_grp, gi])
    v3 = jnp.concatenate([used & r_grp, gu])
    tab3 = pack_table(t3, s3, i3, v3, nloc)
    sq3 = jnp.concatenate([sq_ng, sq_pg], axis=0)
    smoothed = run_phase("final", tab3, t3.shape[0], embeddings, sq_col, [ng, pg], sq3, num, den)
    return smoothed.reshape(total_rows, width)


def solution(mesh):
    placed = (P(("group", "dev"), None), P(("group", "dev"), None), P(("group", "dev")))
    return jax.shard_map(
        local, mesh=mesh, in_specs=placed, out_specs=P(("group", "dev"), None), check_vma=False
    )
```

```python
import jax
import jax.numpy as jnp
from jax import lax
from jax.experimental import pallas as pl
from jax.experimental.pallas import tpu as pltpu
from jax.sharding import PartitionSpec as P

BLOCK = 256
scale_factor = 0.4
VMEM_LIMIT = 56 * 1024 * 1024


def shifted(shard, axis, by):
    devices = lax.axis_size(axis)
    pairs = [(i, i + by) for i in range(devices) if 0 <= i + by < devices]
    return lax.ppermute(shard, axis, pairs)


def squares_of(blocks):
    return jnp.einsum("bsd,bsd->bs", blocks, blocks, preferred_element_type=jnp.float32)


def pack_table(t, s, ix, v, nloc):
    t = jnp.clip(t, 0, nloc - 1)
    ix = jnp.clip(ix, 0, nloc - 1)
    return jnp.stack([t, s, ix, v.astype(jnp.int32)], axis=0).reshape(-1).astype(jnp.int32)


def make_kernel(nsrc, n, mode):
    def kernel(tab, own_ref, sqc_ref, *refs):
        src_refs = refs[:nsrc]
        sqr_ref = refs[nsrc]
        rest = refs[nsrc + 1:]
        if mode == "init":
            num_ref, den_ref = rest
        elif mode == "accum":
            num_in, den_in, num_ref, den_ref = rest
        else:
            num_in, den_in, out_ref, num_ref, den_ref = rest
        nloc = own_ref.shape[0] // BLOCK
        width = own_ref.shape[1]

        if mode == "accum":
            num_ref[...] = num_in[...]
            den_ref[...] = den_in[...]
        else:
            num_ref[...] = jnp.zeros_like(num_ref)
            den_ref[...] = jnp.zeros_like(den_ref)

        def contribute(t, prow, p_ref, ix):
            xt = own_ref[pl.ds(pl.multiple_of(t * BLOCK, BLOCK), BLOCK), :]
            xp = p_ref[pl.ds(pl.multiple_of(ix * BLOCK, BLOCK), BLOCK), :]
            inner = lax.dot_general(xt, xp, (((1,), (1,)), ((), ())),
                                    preferred_element_type=jnp.float32)
            sq_t = sqc_ref[t]
            sq_p = sqr_ref[pl.ds(prow, 1), :]
            distance = sq_t + sq_p - 2.0 * inner
            w = jnp.exp(-distance / (scale_factor * width)).astype(jnp.bfloat16)
            num_ref[t] += jnp.dot(w, xp, preferred_element_type=jnp.float32)
            den_ref[t] += jnp.sum(w.astype(jnp.float32), axis=1, keepdims=True)

        def body(j, carry):
            t = tab[j]
            s = tab[n + j]
            ix = tab[2 * n + j]
            used = tab[3 * n + j] == 1
            for k, p_ref in enumerate(src_refs):
                @pl.when(used & (s == k))
                def _():
                    contribute(t, k * nloc + ix, p_ref, ix)
            return carry

        lax.fori_loop(0, n, body, 0)

        if mode == "final":
            def fin(b, carry):
                out_ref[b] = ((num_in[b] + num_ref[b]) / (den_in[b] + den_ref[b])).astype(
                    out_ref.dtype)
                return carry
            lax.fori_loop(0, nloc, fin, 0)

    return kernel


def run_phase(mode, tab, n, own, sq_col, sources, sq_rows, num=None, den=None):
    rows, width = own.shape
    block = BLOCK
    nloc = rows // block
    nsrc = len(sources)
    vm = pl.BlockSpec(memory_space=pltpu.VMEM)
    in_specs = [pl.BlockSpec(memory_space=pltpu.SMEM), vm, vm] + [vm] * nsrc + [vm]
    args = [tab, own, sq_col, *sources, sq_rows]
    acc_shapes = [jax.ShapeDtypeStruct((nloc, block, width), jnp.float32),
                  jax.ShapeDtypeStruct((nloc, block, 1), jnp.float32)]
    scratch = []
    if mode != "init":
        in_specs += [vm, vm]
        args += [num, den]
    if mode == "final":
        out_shape = jax.ShapeDtypeStruct((nloc, block, width), jnp.bfloat16)
        out_specs = vm
        scratch = [pltpu.VMEM((nloc, block, width), jnp.float32),
                   pltpu.VMEM((nloc, block, 1), jnp.float32)]
    else:
        out_shape = acc_shapes
        out_specs = [vm, vm]
    flops = n * 4 * block * block * width
    return pl.pallas_call(
        make_kernel(nsrc, n, mode),
        in_specs=in_specs,
        out_specs=out_specs,
        out_shape=out_shape,
        scratch_shapes=scratch,
        compiler_params=pltpu.CompilerParams(vmem_limit_bytes=VMEM_LIMIT),
        cost_estimate=pl.CostEstimate(flops=flops, transcendentals=n * block * block,
                                      bytes_accessed=(nsrc + 3) * nloc * block * width * 2),
    )(*args)


def decode_meta(m, nloc, slots):
    nsq = nloc * BLOCK
    sq = m[:nsq].reshape(nloc, BLOCK)
    pairs = m[nsq:nsq + 2 * slots].astype(jnp.int32).reshape(slots, 2)
    count = m[nsq + 2 * slots:].astype(jnp.int32)
    return sq, pairs, count


def local(embeddings, pair_blocks, pair_count):
    total_rows, width = embeddings.shape
    nloc = total_rows // BLOCK
    slots = pair_blocks.shape[0]
    blocks = embeddings.reshape(nloc, BLOCK, width)
    owners = lax.axis_size("dev")
    first_block = (lax.axis_index("group") * owners + lax.axis_index("dev")) * nloc

    nd = shifted(embeddings, "dev", -1)
    pd = shifted(embeddings, "dev", 1)
    ng = shifted(embeddings, "group", -1)
    pg = shifted(embeddings, "group", 1)
    own_sq = squares_of(blocks)
    meta = jnp.concatenate([own_sq.reshape(-1),
                            pair_blocks.reshape(-1).astype(jnp.float32),
                            pair_count.astype(jnp.float32)])
    m_nd = shifted(meta, "dev", -1)
    m_pd = shifted(meta, "dev", 1)
    m_ng = shifted(meta, "group", -1)
    m_pg = shifted(meta, "group", 1)

    pos = jnp.arange(slots, dtype=jnp.int32)
    used = pos < pair_count[0]
    left = pair_blocks[:, 0] - first_block
    right = pair_blocks[:, 1]
    roff = right - first_block
    r_local = roff < nloc
    r_dev = (roff >= nloc) & (roff < 2 * nloc)
    r_grp = ~r_local & ~r_dev
    ridx_dev = roff - nloc
    ridx_grp = right - first_block - owners * nloc
    zeros = jnp.zeros((slots,), jnp.int32)
    ones = jnp.ones((slots,), jnp.int32)
    sq_col = own_sq[:, :, None]

    diag = jnp.arange(nloc, dtype=jnp.int32)
    t1 = jnp.concatenate([diag, left, roff])
    i1 = jnp.concatenate([diag, roff, left])
    v1 = jnp.concatenate([jnp.ones((nloc,), bool), used & r_local, used & r_local])
    tab1 = pack_table(t1, jnp.zeros_like(t1), i1, v1, nloc)
    num, den = run_phase("init", tab1, t1.shape[0], embeddings, sq_col, [embeddings], own_sq)

    def prev_entries(pairs, count, prev_first):
        u = pos < count[0]
        r = pairs[:, 1] - first_block
        u = u & (r >= 0) & (r < nloc)
        return r, pairs[:, 0] - prev_first, u

    nd, pd, m_nd, m_pd, num, den = lax.optimization_barrier((nd, pd, m_nd, m_pd, num, den))
    sq_nd, _, _ = decode_meta(m_nd, nloc, slots)
    sq_pd, pd_pairs, pd_count = decode_meta(m_pd, nloc, slots)
    pr, pi, pu = prev_entries(pd_pairs, pd_count, first_block - nloc)
    t2 = jnp.concatenate([left, pr])
    s2 = jnp.concatenate([zeros, ones])
    i2 = jnp.concatenate([ridx_dev, pi])
    v2 = jnp.concatenate([used & r_dev, pu])
    tab2 = pack_table(t2, s2, i2, v2, nloc)
    sq2 = jnp.concatenate([sq_nd, sq_pd], axis=0)
    num, den = run_phase("accum", tab2, t2.shape[0], embeddings, sq_col, [nd, pd], sq2, num, den)

    ng, pg, m_ng, m_pg, num, den = lax.optimization_barrier((ng, pg, m_ng, m_pg, num, den))
    sq_ng, _, _ = decode_meta(m_ng, nloc, slots)
    sq_pg, pg_pairs, pg_count = decode_meta(m_pg, nloc, slots)
    gr, gi, gu = prev_entries(pg_pairs, pg_count, first_block - owners * nloc)
    t3 = jnp.concatenate([left, gr])
    s3 = jnp.concatenate([zeros, ones])
    i3 = jnp.concatenate([ridx_grp, gi])
    v3 = jnp.concatenate([used & r_grp, gu])
    tab3 = pack_table(t3, s3, i3, v3, nloc)
    sq3 = jnp.concatenate([sq_ng, sq_pg], axis=0)
    smoothed = run_phase("final", tab3, t3.shape[0], embeddings, sq_col, [ng, pg], sq3, num, den)
    return smoothed.reshape(total_rows, width)


def solution(mesh):
    placed = (P(("group", "dev"), None), P(("group", "dev"), None), P(("group", "dev")))
    return jax.shard_map(
        local, mesh=mesh, in_specs=placed, out_specs=P(("group", "dev"), None), check_vma=False
    )
```

```python
import jax
import jax.numpy as jnp
from jax import lax
from jax.experimental import pallas as pl
from jax.experimental.pallas import tpu as pltpu
from jax.sharding import PartitionSpec as P

BLOCK = 256
scale_factor = 0.4
VMEM_LIMIT = 56 * 1024 * 1024


def shifted(shard, axis, by):
    devices = lax.axis_size(axis)
    pairs = [(i, i + by) for i in range(devices) if 0 <= i + by < devices]
    return lax.ppermute(shard, axis, pairs)


def squares_of(blocks):
    return jnp.einsum("bsd,bsd->bs", blocks, blocks, preferred_element_type=jnp.float32)


def pack_table(t, s, ix, v, nloc):
    t = jnp.clip(t, 0, nloc - 1)
    ix = jnp.clip(ix, 0, nloc - 1)
    return jnp.stack([t, s, ix, v.astype(jnp.int32)], axis=0).reshape(-1).astype(jnp.int32)


def make_kernel(nsrc, n, mode):
    def kernel(tab, own_ref, sqc_ref, *refs):
        src_refs = refs[:nsrc]
        sqr_ref = refs[nsrc]
        rest = refs[nsrc + 1:]
        if mode == "init":
            num_ref, den_ref = rest
        elif mode == "accum":
            num_in, den_in, num_ref, den_ref = rest
        else:
            num_in, den_in, out_ref, num_ref, den_ref = rest
        nloc = own_ref.shape[0] // BLOCK
        width = own_ref.shape[1]

        if mode != "init":
            num_ref[...] = num_in[...]
            den_ref[...] = den_in[...]
        else:
            num_ref[...] = jnp.zeros_like(num_ref)
            den_ref[...] = jnp.zeros_like(den_ref)

        def contribute(t, prow, p_ref, ix):
            xt = own_ref[pl.ds(pl.multiple_of(t * BLOCK, BLOCK), BLOCK), :]
            xp = p_ref[pl.ds(pl.multiple_of(ix * BLOCK, BLOCK), BLOCK), :]
            inner = lax.dot_general(xt, xp, (((1,), (1,)), ((), ())),
                                    preferred_element_type=jnp.float32)
            sq_t = sqc_ref[t]
            sq_p = sqr_ref[pl.ds(prow, 1), :]
            distance = sq_t + sq_p - 2.0 * inner
            w = jnp.exp(-distance / (scale_factor * width)).astype(jnp.bfloat16)
            num_ref[t] += jnp.dot(w, xp, preferred_element_type=jnp.float32)
            den_ref[t] += jnp.sum(w.astype(jnp.float32), axis=1, keepdims=True)

        def body(j, carry):
            t = tab[j]
            s = tab[n + j]
            ix = tab[2 * n + j]
            used = tab[3 * n + j] == 1
            for k, p_ref in enumerate(src_refs):
                @pl.when(used & (s == k))
                def _():
                    contribute(t, k * nloc + ix, p_ref, ix)
            return carry

        lax.fori_loop(0, n, body, 0)

        if mode == "final":
            def fin(b, carry):
                out_ref[b] = (num_ref[b] / den_ref[b]).astype(out_ref.dtype)
                return carry
            lax.fori_loop(0, nloc, fin, 0)

    return kernel


def run_phase(mode, tab, n, own, sq_col, sources, sq_rows, num=None, den=None):
    rows, width = own.shape
    block = BLOCK
    nloc = rows // block
    nsrc = len(sources)
    vm = pl.BlockSpec(memory_space=pltpu.VMEM)
    in_specs = [pl.BlockSpec(memory_space=pltpu.SMEM), vm, vm] + [vm] * nsrc + [vm]
    args = [tab, own, sq_col, *sources, sq_rows]
    acc_shapes = [jax.ShapeDtypeStruct((nloc, block, width), jnp.float32),
                  jax.ShapeDtypeStruct((nloc, block, 1), jnp.float32)]
    scratch = []
    if mode != "init":
        in_specs += [vm, vm]
        args += [num, den]
    if mode == "final":
        out_shape = jax.ShapeDtypeStruct((nloc, block, width), jnp.bfloat16)
        out_specs = vm
        scratch = [pltpu.VMEM((nloc, block, width), jnp.float32),
                   pltpu.VMEM((nloc, block, 1), jnp.float32)]
    else:
        out_shape = acc_shapes
        out_specs = [vm, vm]
    flops = n * 4 * block * block * width
    return pl.pallas_call(
        make_kernel(nsrc, n, mode),
        in_specs=in_specs,
        out_specs=out_specs,
        out_shape=out_shape,
        scratch_shapes=scratch,
        compiler_params=pltpu.CompilerParams(vmem_limit_bytes=VMEM_LIMIT),
        cost_estimate=pl.CostEstimate(flops=flops, transcendentals=n * block * block,
                                      bytes_accessed=(nsrc + 3) * nloc * block * width * 2),
    )(*args)


def decode_meta(m, nloc, slots):
    nsq = nloc * BLOCK
    sq = m[:nsq].reshape(nloc, BLOCK)
    pairs = m[nsq:nsq + 2 * slots].astype(jnp.int32).reshape(slots, 2)
    count = m[nsq + 2 * slots:].astype(jnp.int32)
    return sq, pairs, count


def local(embeddings, pair_blocks, pair_count):
    total_rows, width = embeddings.shape
    nloc = total_rows // BLOCK
    slots = pair_blocks.shape[0]
    blocks = embeddings.reshape(nloc, BLOCK, width)
    owners = lax.axis_size("dev")
    first_block = (lax.axis_index("group") * owners + lax.axis_index("dev")) * nloc

    nd = shifted(embeddings, "dev", -1)
    pd = shifted(embeddings, "dev", 1)
    ng = shifted(embeddings, "group", -1)
    pg = shifted(embeddings, "group", 1)
    own_sq = squares_of(blocks)
    meta = jnp.concatenate([own_sq.reshape(-1),
                            pair_blocks.reshape(-1).astype(jnp.float32),
                            pair_count.astype(jnp.float32)])
    m_nd = shifted(meta, "dev", -1)
    m_pd = shifted(meta, "dev", 1)
    m_ng = shifted(meta, "group", -1)
    m_pg = shifted(meta, "group", 1)

    pos = jnp.arange(slots, dtype=jnp.int32)
    used = pos < pair_count[0]
    left = pair_blocks[:, 0] - first_block
    right = pair_blocks[:, 1]
    roff = right - first_block
    r_local = roff < nloc
    r_dev = (roff >= nloc) & (roff < 2 * nloc)
    r_grp = ~r_local & ~r_dev
    ridx_dev = roff - nloc
    ridx_grp = right - first_block - owners * nloc
    zeros = jnp.zeros((slots,), jnp.int32)
    ones = jnp.ones((slots,), jnp.int32)
    sq_col = own_sq[:, :, None]

    diag = jnp.arange(nloc, dtype=jnp.int32)
    t1 = jnp.concatenate([diag, left, roff])
    i1 = jnp.concatenate([diag, roff, left])
    v1 = jnp.concatenate([jnp.ones((nloc,), bool), used & r_local, used & r_local])
    tab1 = pack_table(t1, jnp.zeros_like(t1), i1, v1, nloc)
    num, den = run_phase("init", tab1, t1.shape[0], embeddings, sq_col, [embeddings], own_sq)

    def prev_entries(pairs, count, prev_first):
        u = pos < count[0]
        r = pairs[:, 1] - first_block
        u = u & (r >= 0) & (r < nloc)
        return r, pairs[:, 0] - prev_first, u

    nd, pd, m_nd, m_pd, num, den = lax.optimization_barrier((nd, pd, m_nd, m_pd, num, den))
    sq_nd, _, _ = decode_meta(m_nd, nloc, slots)
    sq_pd, pd_pairs, pd_count = decode_meta(m_pd, nloc, slots)
    pr, pi, pu = prev_entries(pd_pairs, pd_count, first_block - nloc)
    t2 = jnp.concatenate([left, pr])
    s2 = jnp.concatenate([zeros, ones])
    i2 = jnp.concatenate([ridx_dev, pi])
    v2 = jnp.concatenate([used & r_dev, pu])
    tab2 = pack_table(t2, s2, i2, v2, nloc)
    sq2 = jnp.concatenate([sq_nd, sq_pd], axis=0)
    num, den = run_phase("accum", tab2, t2.shape[0], embeddings, sq_col, [nd, pd], sq2, num, den)

    ng, pg, m_ng, m_pg, num, den = lax.optimization_barrier((ng, pg, m_ng, m_pg, num, den))
    sq_ng, _, _ = decode_meta(m_ng, nloc, slots)
    sq_pg, pg_pairs, pg_count = decode_meta(m_pg, nloc, slots)
    gr, gi, gu = prev_entries(pg_pairs, pg_count, first_block - owners * nloc)
    t3 = jnp.concatenate([left, gr])
    s3 = jnp.concatenate([zeros, ones])
    i3 = jnp.concatenate([ridx_grp, gi])
    v3 = jnp.concatenate([used & r_grp, gu])
    tab3 = pack_table(t3, s3, i3, v3, nloc)
    sq3 = jnp.concatenate([sq_ng, sq_pg], axis=0)
    smoothed = run_phase("final", tab3, t3.shape[0], embeddings, sq_col, [ng, pg], sq3, num, den)
    return smoothed.reshape(total_rows, width)


def solution(mesh):
    placed = (P(("group", "dev"), None), P(("group", "dev"), None), P(("group", "dev")))
    return jax.shard_map(
        local, mesh=mesh, in_specs=placed, out_specs=P(("group", "dev"), None), check_vma=False
    )
```

```python
import jax
import jax.numpy as jnp
from jax import lax
from jax.experimental import pallas as pl
from jax.experimental.pallas import tpu as pltpu
from jax.sharding import PartitionSpec as P

BLOCK = 256
scale_factor = 0.4
VMEM_LIMIT = 56 * 1024 * 1024


def shifted(shard, axis, by):
    devices = lax.axis_size(axis)
    pairs = [(i, i + by) for i in range(devices) if 0 <= i + by < devices]
    return lax.ppermute(shard, axis, pairs)


def squares_of(blocks):
    return jnp.einsum("bsd,bsd->bs", blocks, blocks, preferred_element_type=jnp.float32)


def pack_table(t, s, ix, v, nloc):
    t = jnp.clip(t, 0, nloc - 1)
    ix = jnp.clip(ix, 0, nloc - 1)
    return jnp.stack([t, s, ix, v.astype(jnp.int32)], axis=0).reshape(-1).astype(jnp.int32)


def make_kernel(nsrc, n, mode):
    def kernel(tab, own_ref, sqc_ref, *refs):
        src_refs = refs[:nsrc]
        sqr_ref = refs[nsrc]
        rest = refs[nsrc + 1:]
        if mode == "init":
            num_ref, den_ref = rest
        elif mode == "accum":
            num_in, den_in, num_ref, den_ref = rest
        else:
            num_in, den_in, out_ref, num_ref, den_ref, stage, out_sem = rest
        nloc = own_ref.shape[0] // BLOCK
        width = own_ref.shape[1]

        if mode != "init":
            num_ref[...] = num_in[...]
            den_ref[...] = den_in[...]
        else:
            num_ref[...] = jnp.zeros_like(num_ref)
            den_ref[...] = jnp.zeros_like(den_ref)

        def contribute(t, prow, p_ref, ix):
            xt = own_ref[pl.ds(pl.multiple_of(t * BLOCK, BLOCK), BLOCK), :]
            xp = p_ref[pl.ds(pl.multiple_of(ix * BLOCK, BLOCK), BLOCK), :]
            inner = lax.dot_general(xt, xp, (((1,), (1,)), ((), ())),
                                    preferred_element_type=jnp.float32)
            sq_t = sqc_ref[t]
            sq_p = sqr_ref[pl.ds(prow, 1), :]
            distance = sq_t + sq_p - 2.0 * inner
            w = jnp.exp(-distance / (scale_factor * width)).astype(jnp.bfloat16)
            num_ref[t] += jnp.dot(w, xp, preferred_element_type=jnp.float32)
            den_ref[t] += jnp.sum(w.astype(jnp.float32), axis=1, keepdims=True)

        def body(j, carry):
            t = tab[j]
            s = tab[n + j]
            ix = tab[2 * n + j]
            used = tab[3 * n + j] == 1
            for k, p_ref in enumerate(src_refs):
                @pl.when(used & (s == k))
                def _():
                    contribute(t, k * nloc + ix, p_ref, ix)
            return carry

        lax.fori_loop(0, n, body, 0)

        if mode == "final":
            copies = []
            for b in range(nloc):
                stage[b] = (num_ref[b] / den_ref[b]).astype(stage.dtype)
                cp = pltpu.make_async_copy(stage.at[b], out_ref.at[b], out_sem.at[b])
                cp.start()
                copies.append(cp)
            for cp in copies:
                cp.wait()

    return kernel


def run_phase(mode, tab, n, own, sq_col, sources, sq_rows, num=None, den=None):
    rows, width = own.shape
    block = BLOCK
    nloc = rows // block
    nsrc = len(sources)
    vm = pl.BlockSpec(memory_space=pltpu.VMEM)
    in_specs = [pl.BlockSpec(memory_space=pltpu.SMEM), vm, vm] + [vm] * nsrc + [vm]
    args = [tab, own, sq_col, *sources, sq_rows]
    acc_shapes = [jax.ShapeDtypeStruct((nloc, block, width), jnp.float32),
                  jax.ShapeDtypeStruct((nloc, block, 1), jnp.float32)]
    scratch = []
    if mode != "init":
        in_specs += [vm, vm]
        args += [num, den]
    if mode == "final":
        out_shape = jax.ShapeDtypeStruct((nloc, block, width), jnp.bfloat16)
        out_specs = pl.BlockSpec(memory_space=pl.ANY)
        scratch = [pltpu.VMEM((nloc, block, width), jnp.float32),
                   pltpu.VMEM((nloc, block, 1), jnp.float32),
                   pltpu.VMEM((nloc, block, width), jnp.bfloat16),
                   pltpu.SemaphoreType.DMA((nloc,))]
    else:
        out_shape = acc_shapes
        out_specs = [vm, vm]
    flops = n * 4 * block * block * width
    return pl.pallas_call(
        make_kernel(nsrc, n, mode),
        in_specs=in_specs,
        out_specs=out_specs,
        out_shape=out_shape,
        scratch_shapes=scratch,
        compiler_params=pltpu.CompilerParams(vmem_limit_bytes=VMEM_LIMIT),
        cost_estimate=pl.CostEstimate(flops=flops, transcendentals=n * block * block,
                                      bytes_accessed=(nsrc + 3) * nloc * block * width * 2),
    )(*args)


def decode_meta(m, nloc, slots):
    nsq = nloc * BLOCK
    sq = m[:nsq].reshape(nloc, BLOCK)
    pairs = m[nsq:nsq + 2 * slots].astype(jnp.int32).reshape(slots, 2)
    count = m[nsq + 2 * slots:].astype(jnp.int32)
    return sq, pairs, count


def local(embeddings, pair_blocks, pair_count):
    total_rows, width = embeddings.shape
    nloc = total_rows // BLOCK
    slots = pair_blocks.shape[0]
    blocks = embeddings.reshape(nloc, BLOCK, width)
    owners = lax.axis_size("dev")
    first_block = (lax.axis_index("group") * owners + lax.axis_index("dev")) * nloc

    nd = shifted(embeddings, "dev", -1)
    pd = shifted(embeddings, "dev", 1)
    ng = shifted(embeddings, "group", -1)
    pg = shifted(embeddings, "group", 1)
    own_sq = squares_of(blocks)
    meta = jnp.concatenate([own_sq.reshape(-1),
                            pair_blocks.reshape(-1).astype(jnp.float32),
                            pair_count.astype(jnp.float32)])
    m_nd = shifted(meta, "dev", -1)
    m_pd = shifted(meta, "dev", 1)
    m_ng = shifted(meta, "group", -1)
    m_pg = shifted(meta, "group", 1)

    pos = jnp.arange(slots, dtype=jnp.int32)
    used = pos < pair_count[0]
    left = pair_blocks[:, 0] - first_block
    right = pair_blocks[:, 1]
    roff = right - first_block
    r_local = roff < nloc
    r_dev = (roff >= nloc) & (roff < 2 * nloc)
    r_grp = ~r_local & ~r_dev
    ridx_dev = roff - nloc
    ridx_grp = right - first_block - owners * nloc
    zeros = jnp.zeros((slots,), jnp.int32)
    ones = jnp.ones((slots,), jnp.int32)
    sq_col = own_sq[:, :, None]

    diag = jnp.arange(nloc, dtype=jnp.int32)
    t1 = jnp.concatenate([diag, left, roff])
    i1 = jnp.concatenate([diag, roff, left])
    v1 = jnp.concatenate([jnp.ones((nloc,), bool), used & r_local, used & r_local])
    tab1 = pack_table(t1, jnp.zeros_like(t1), i1, v1, nloc)
    num, den = run_phase("init", tab1, t1.shape[0], embeddings, sq_col, [embeddings], own_sq)

    def prev_entries(pairs, count, prev_first):
        u = pos < count[0]
        r = pairs[:, 1] - first_block
        u = u & (r >= 0) & (r < nloc)
        return r, pairs[:, 0] - prev_first, u

    nd, pd, m_nd, m_pd, num, den = lax.optimization_barrier((nd, pd, m_nd, m_pd, num, den))
    sq_nd, _, _ = decode_meta(m_nd, nloc, slots)
    sq_pd, pd_pairs, pd_count = decode_meta(m_pd, nloc, slots)
    pr, pi, pu = prev_entries(pd_pairs, pd_count, first_block - nloc)
    t2 = jnp.concatenate([left, pr])
    s2 = jnp.concatenate([zeros, ones])
    i2 = jnp.concatenate([ridx_dev, pi])
    v2 = jnp.concatenate([used & r_dev, pu])
    tab2 = pack_table(t2, s2, i2, v2, nloc)
    sq2 = jnp.concatenate([sq_nd, sq_pd], axis=0)
    num, den = run_phase("accum", tab2, t2.shape[0], embeddings, sq_col, [nd, pd], sq2, num, den)

    ng, pg, m_ng, m_pg, num, den = lax.optimization_barrier((ng, pg, m_ng, m_pg, num, den))
    sq_ng, _, _ = decode_meta(m_ng, nloc, slots)
    sq_pg, pg_pairs, pg_count = decode_meta(m_pg, nloc, slots)
    gr, gi, gu = prev_entries(pg_pairs, pg_count, first_block - owners * nloc)
    t3 = jnp.concatenate([left, gr])
    s3 = jnp.concatenate([zeros, ones])
    i3 = jnp.concatenate([ridx_grp, gi])
    v3 = jnp.concatenate([used & r_grp, gu])
    tab3 = pack_table(t3, s3, i3, v3, nloc)
    sq3 = jnp.concatenate([sq_ng, sq_pg], axis=0)
    smoothed = run_phase("final", tab3, t3.shape[0], embeddings, sq_col, [ng, pg], sq3, num, den)
    return smoothed.reshape(total_rows, width)


def solution(mesh):
    placed = (P(("group", "dev"), None), P(("group", "dev"), None), P(("group", "dev")))
    return jax.shard_map(
        local, mesh=mesh, in_specs=placed, out_specs=P(("group", "dev"), None), check_vma=False
    )
```

```python
import jax
import jax.numpy as jnp
from jax import lax
from jax.experimental import pallas as pl
from jax.experimental.pallas import tpu as pltpu
from jax.sharding import PartitionSpec as P

BLOCK = 256
scale_factor = 0.4
VMEM_LIMIT = 56 * 1024 * 1024


def shifted(shard, axis, by):
    devices = lax.axis_size(axis)
    pairs = [(i, i + by) for i in range(devices) if 0 <= i + by < devices]
    return lax.ppermute(shard, axis, pairs)


def squares_of(blocks):
    return jnp.einsum("bsd,bsd->bs", blocks, blocks, preferred_element_type=jnp.float32)


def pack_table(t, s, ix, v, nloc):
    t = jnp.clip(t, 0, nloc - 1)
    ix = jnp.clip(ix, 0, nloc - 1)
    return jnp.stack([t, s, ix, v.astype(jnp.int32)], axis=0).reshape(-1).astype(jnp.int32)


def make_kernel(nsrc, n, mode):
    def kernel(tab, own_ref, ownt_ref, sqc_ref, *refs):
        src_refs = refs[:nsrc]
        sqr_ref = refs[nsrc]
        rest = refs[nsrc + 1:]
        if mode == "init":
            num_ref, den_ref = rest
        elif mode == "accum":
            num_in, den_in, num_ref, den_ref = rest
        else:
            num_in, den_in, out_ref, num_ref, den_ref = rest
        nloc = own_ref.shape[0] // BLOCK
        width = own_ref.shape[1]

        if mode != "init":
            num_ref[...] = num_in[...]
            den_ref[...] = den_in[...]
        else:
            num_ref[...] = jnp.zeros_like(num_ref)
            den_ref[...] = jnp.zeros_like(den_ref)

        def contribute(t, prow, p_ref, ix):
            xt_t = ownt_ref[:, pl.ds(pl.multiple_of(t * BLOCK, BLOCK), BLOCK)]
            xp = p_ref[pl.ds(pl.multiple_of(ix * BLOCK, BLOCK), BLOCK), :]
            inner_t = jnp.dot(xp, xt_t, preferred_element_type=jnp.float32)
            sq_t = sqc_ref[pl.ds(t, 1), :]
            sq_p = sqr_ref[prow]
            distance = sq_p + sq_t - 2.0 * inner_t
            w_t = jnp.exp(-distance / (scale_factor * width)).astype(jnp.bfloat16)
            num_ref[t] += lax.dot_general(w_t, xp, (((0,), (0,)), ((), ())),
                                          preferred_element_type=jnp.float32)
            den_ref[t] += jnp.sum(w_t.astype(jnp.float32), axis=0, keepdims=True)

        def body(j, carry):
            t = tab[j]
            s = tab[n + j]
            ix = tab[2 * n + j]
            used = tab[3 * n + j] == 1
            for k, p_ref in enumerate(src_refs):
                @pl.when(used & (s == k))
                def _():
                    contribute(t, k * nloc + ix, p_ref, ix)
            return carry

        lax.fori_loop(0, n, body, 0)

        if mode == "final":
            def fin(b, carry):
                dcol = jnp.transpose(jnp.broadcast_to(den_ref[b], (8, BLOCK)), (1, 0))[:, 0:1]
                out_ref[b] = (num_ref[b] / dcol).astype(out_ref.dtype)
                return carry
            lax.fori_loop(0, nloc, fin, 0)

    return kernel


def run_phase(mode, tab, n, own, own_t, sq_row, sources, sq_cols, num=None, den=None):
    rows, width = own.shape
    block = BLOCK
    nloc = rows // block
    nsrc = len(sources)
    vm = pl.BlockSpec(memory_space=pltpu.VMEM)
    in_specs = [pl.BlockSpec(memory_space=pltpu.SMEM), vm, vm, vm] + [vm] * nsrc + [vm]
    args = [tab, own, own_t, sq_row, *sources, sq_cols]
    acc_shapes = [jax.ShapeDtypeStruct((nloc, block, width), jnp.float32),
                  jax.ShapeDtypeStruct((nloc, 1, block), jnp.float32)]
    scratch = []
    if mode != "init":
        in_specs += [vm, vm]
        args += [num, den]
    if mode == "final":
        out_shape = jax.ShapeDtypeStruct((nloc, block, width), jnp.bfloat16)
        out_specs = vm
        scratch = [pltpu.VMEM((nloc, block, width), jnp.float32),
                   pltpu.VMEM((nloc, 1, block), jnp.float32)]
    else:
        out_shape = acc_shapes
        out_specs = [vm, vm]
    flops = n * 4 * block * block * width
    return pl.pallas_call(
        make_kernel(nsrc, n, mode),
        in_specs=in_specs,
        out_specs=out_specs,
        out_shape=out_shape,
        scratch_shapes=scratch,
        compiler_params=pltpu.CompilerParams(vmem_limit_bytes=VMEM_LIMIT),
        cost_estimate=pl.CostEstimate(flops=flops, transcendentals=n * block * block,
                                      bytes_accessed=(nsrc + 3) * nloc * block * width * 2),
    )(*args)


def decode_meta(m, nloc, slots):
    nsq = nloc * BLOCK
    sq = m[:nsq].reshape(nloc, BLOCK)
    pairs = m[nsq:nsq + 2 * slots].astype(jnp.int32).reshape(slots, 2)
    count = m[nsq + 2 * slots:].astype(jnp.int32)
    return sq, pairs, count


def local(embeddings, pair_blocks, pair_count):
    total_rows, width = embeddings.shape
    nloc = total_rows // BLOCK
    slots = pair_blocks.shape[0]
    blocks = embeddings.reshape(nloc, BLOCK, width)
    owners = lax.axis_size("dev")
    first_block = (lax.axis_index("group") * owners + lax.axis_index("dev")) * nloc

    nd = shifted(embeddings, "dev", -1)
    pd = shifted(embeddings, "dev", 1)
    ng = shifted(embeddings, "group", -1)
    pg = shifted(embeddings, "group", 1)
    own_sq = squares_of(blocks)
    meta = jnp.concatenate([own_sq.reshape(-1),
                            pair_blocks.reshape(-1).astype(jnp.float32),
                            pair_count.astype(jnp.float32)])
    m_nd = shifted(meta, "dev", -1)
    m_pd = shifted(meta, "dev", 1)
    m_ng = shifted(meta, "group", -1)
    m_pg = shifted(meta, "group", 1)

    pos = jnp.arange(slots, dtype=jnp.int32)
    used = pos < pair_count[0]
    left = pair_blocks[:, 0] - first_block
    right = pair_blocks[:, 1]
    roff = right - first_block
    r_local = roff < nloc
    r_dev = (roff >= nloc) & (roff < 2 * nloc)
    r_grp = ~r_local & ~r_dev
    ridx_dev = roff - nloc
    ridx_grp = right - first_block - owners * nloc
    zeros = jnp.zeros((slots,), jnp.int32)
    ones = jnp.ones((slots,), jnp.int32)
    own_t = embeddings.T

    diag = jnp.arange(nloc, dtype=jnp.int32)
    t1 = jnp.concatenate([diag, left, roff])
    i1 = jnp.concatenate([diag, roff, left])
    v1 = jnp.concatenate([jnp.ones((nloc,), bool), used & r_local, used & r_local])
    tab1 = pack_table(t1, jnp.zeros_like(t1), i1, v1, nloc)
    num, den = run_phase("init", tab1, t1.shape[0], embeddings, own_t, own_sq, [embeddings],
                         own_sq[:, :, None])

    def prev_entries(pairs, count, prev_first):
        u = pos < count[0]
        r = pairs[:, 1] - first_block
        u = u & (r >= 0) & (r < nloc)
        return r, pairs[:, 0] - prev_first, u

    nd, pd, m_nd, m_pd, num, den = lax.optimization_barrier((nd, pd, m_nd, m_pd, num, den))
    sq_nd, _, _ = decode_meta(m_nd, nloc, slots)
    sq_pd, pd_pairs, pd_count = decode_meta(m_pd, nloc, slots)
    pr, pi, pu = prev_entries(pd_pairs, pd_count, first_block - nloc)
    t2 = jnp.concatenate([left, pr])
    s2 = jnp.concatenate([zeros, ones])
    i2 = jnp.concatenate([ridx_dev, pi])
    v2 = jnp.concatenate([used & r_dev, pu])
    tab2 = pack_table(t2, s2, i2, v2, nloc)
    sq2 = jnp.concatenate([sq_nd, sq_pd], axis=0)
    num, den = run_phase("accum", tab2, t2.shape[0], embeddings, own_t, own_sq, [nd, pd],
                         sq2[:, :, None], num, den)

    ng, pg, m_ng, m_pg, num, den = lax.optimization_barrier((ng, pg, m_ng, m_pg, num, den))
    sq_ng, _, _ = decode_meta(m_ng, nloc, slots)
    sq_pg, pg_pairs, pg_count = decode_meta(m_pg, nloc, slots)
    gr, gi, gu = prev_entries(pg_pairs, pg_count, first_block - owners * nloc)
    t3 = jnp.concatenate([left, gr])
    s3 = jnp.concatenate([zeros, ones])
    i3 = jnp.concatenate([ridx_grp, gi])
    v3 = jnp.concatenate([used & r_grp, gu])
    tab3 = pack_table(t3, s3, i3, v3, nloc)
    sq3 = jnp.concatenate([sq_ng, sq_pg], axis=0)
    smoothed = run_phase("final", tab3, t3.shape[0], embeddings, own_t, own_sq, [ng, pg],
                         sq3[:, :, None], num, den)
    return smoothed.reshape(total_rows, width)


def solution(mesh):
    placed = (P(("group", "dev"), None), P(("group", "dev"), None), P(("group", "dev")))
    return jax.shard_map(
        local, mesh=mesh, in_specs=placed, out_specs=P(("group", "dev"), None), check_vma=False
    )
```

```python
import jax
import jax.numpy as jnp
from jax import lax
from jax.experimental import pallas as pl
from jax.experimental.pallas import tpu as pltpu
from jax.sharding import PartitionSpec as P

BLOCK = 256
scale_factor = 0.4
VMEM_LIMIT = 56 * 1024 * 1024


def shifted(shard, axis, by):
    devices = lax.axis_size(axis)
    pairs = [(i, i + by) for i in range(devices) if 0 <= i + by < devices]
    return lax.ppermute(shard, axis, pairs)


def squares_of(blocks):
    return jnp.einsum("bsd,bsd->bs", blocks, blocks, preferred_element_type=jnp.float32)


def pack_table(t, s, ix, v, nloc):
    t = jnp.clip(t, 0, nloc - 1)
    ix = jnp.clip(ix, 0, nloc - 1)
    return jnp.stack([t, s, ix, v.astype(jnp.int32)], axis=0).reshape(-1).astype(jnp.int32)


def make_kernel(nsrc, n, mode):
    def kernel(tab, own_ref, sqc_ref, *refs):
        src_refs = refs[:nsrc]
        sqr_ref = refs[nsrc]
        rest = refs[nsrc + 1:]
        if mode == "init":
            num_ref, den_ref = rest
        elif mode == "accum":
            num_in, den_in, num_ref, den_ref = rest
        else:
            num_in, den_in, out_ref, num_ref, den_ref = rest
        nloc = own_ref.shape[0] // BLOCK
        width = own_ref.shape[1]

        if mode != "init":
            num_ref[...] = num_in[...]
            den_ref[...] = den_in[...]
        else:
            num_ref[...] = jnp.zeros_like(num_ref)
            den_ref[...] = jnp.zeros_like(den_ref)

        def contribute(t, prow, p_ref, ix):
            xt = own_ref[pl.ds(pl.multiple_of(t * BLOCK, BLOCK), BLOCK), :]
            xp = p_ref[pl.ds(pl.multiple_of(ix * BLOCK, BLOCK), BLOCK), :]
            inner = lax.dot_general(xt, xp, (((1,), (1,)), ((), ())),
                                    preferred_element_type=jnp.float32)
            sq_t = sqc_ref[t]
            sq_p = sqr_ref[pl.ds(prow, 1), :]
            distance = sq_t + sq_p - 2.0 * inner
            w = jnp.exp(-distance / (scale_factor * width)).astype(jnp.bfloat16)
            num_ref[t] += jnp.dot(w, xp, preferred_element_type=jnp.float32)
            den_ref[t] += jnp.sum(w.astype(jnp.float32), axis=1, keepdims=True)

        def body(j, carry):
            t = tab[j]
            s = tab[n + j]
            ix = tab[2 * n + j]
            used = tab[3 * n + j] == 1
            for k, p_ref in enumerate(src_refs):
                @pl.when(used & (s == k))
                def _():
                    contribute(t, k * nloc + ix, p_ref, ix)
            return carry

        lax.fori_loop(0, n, body, 0)

        if mode == "final":
            def fin(b, carry):
                inv = 1.0 / den_ref[b]
                out_ref[b] = (num_ref[b] * inv).astype(out_ref.dtype)
                return carry
            lax.fori_loop(0, nloc, fin, 0)

    return kernel


def run_phase(mode, tab, n, own, sq_col, sources, sq_rows, num=None, den=None):
    rows, width = own.shape
    block = BLOCK
    nloc = rows // block
    nsrc = len(sources)
    vm = pl.BlockSpec(memory_space=pltpu.VMEM)
    in_specs = [pl.BlockSpec(memory_space=pltpu.SMEM), vm, vm] + [vm] * nsrc + [vm]
    args = [tab, own, sq_col, *sources, sq_rows]
    acc_shapes = [jax.ShapeDtypeStruct((nloc, block, width), jnp.float32),
                  jax.ShapeDtypeStruct((nloc, block, 1), jnp.float32)]
    scratch = []
    if mode != "init":
        in_specs += [vm, vm]
        args += [num, den]
    if mode == "final":
        out_shape = jax.ShapeDtypeStruct((nloc, block, width), jnp.bfloat16)
        out_specs = vm
        scratch = [pltpu.VMEM((nloc, block, width), jnp.float32),
                   pltpu.VMEM((nloc, block, 1), jnp.float32)]
    else:
        out_shape = acc_shapes
        out_specs = [vm, vm]
    flops = n * 4 * block * block * width
    return pl.pallas_call(
        make_kernel(nsrc, n, mode),
        in_specs=in_specs,
        out_specs=out_specs,
        out_shape=out_shape,
        scratch_shapes=scratch,
        compiler_params=pltpu.CompilerParams(vmem_limit_bytes=VMEM_LIMIT),
        cost_estimate=pl.CostEstimate(flops=flops, transcendentals=n * block * block,
                                      bytes_accessed=(nsrc + 3) * nloc * block * width * 2),
    )(*args)


def decode_meta(m, nloc, slots):
    nsq = nloc * BLOCK
    sq = m[:nsq].reshape(nloc, BLOCK)
    pairs = m[nsq:nsq + 2 * slots].astype(jnp.int32).reshape(slots, 2)
    count = m[nsq + 2 * slots:].astype(jnp.int32)
    return sq, pairs, count


def local(embeddings, pair_blocks, pair_count):
    total_rows, width = embeddings.shape
    nloc = total_rows // BLOCK
    slots = pair_blocks.shape[0]
    blocks = embeddings.reshape(nloc, BLOCK, width)
    owners = lax.axis_size("dev")
    first_block = (lax.axis_index("group") * owners + lax.axis_index("dev")) * nloc

    nd = shifted(embeddings, "dev", -1)
    pd = shifted(embeddings, "dev", 1)
    ng = shifted(embeddings, "group", -1)
    pg = shifted(embeddings, "group", 1)
    own_sq = squares_of(blocks)
    meta = jnp.concatenate([own_sq.reshape(-1),
                            pair_blocks.reshape(-1).astype(jnp.float32),
                            pair_count.astype(jnp.float32)])
    m_nd = shifted(meta, "dev", -1)
    m_pd = shifted(meta, "dev", 1)
    m_ng = shifted(meta, "group", -1)
    m_pg = shifted(meta, "group", 1)

    pos = jnp.arange(slots, dtype=jnp.int32)
    used = pos < pair_count[0]
    left = pair_blocks[:, 0] - first_block
    right = pair_blocks[:, 1]
    roff = right - first_block
    r_local = roff < nloc
    r_dev = (roff >= nloc) & (roff < 2 * nloc)
    r_grp = ~r_local & ~r_dev
    ridx_dev = roff - nloc
    ridx_grp = right - first_block - owners * nloc
    zeros = jnp.zeros((slots,), jnp.int32)
    ones = jnp.ones((slots,), jnp.int32)
    sq_col = own_sq[:, :, None]

    diag = jnp.arange(nloc, dtype=jnp.int32)
    t1 = jnp.concatenate([diag, left, roff])
    i1 = jnp.concatenate([diag, roff, left])
    v1 = jnp.concatenate([jnp.ones((nloc,), bool), used & r_local, used & r_local])
    tab1 = pack_table(t1, jnp.zeros_like(t1), i1, v1, nloc)
    num, den = run_phase("init", tab1, t1.shape[0], embeddings, sq_col, [embeddings], own_sq)

    def prev_entries(pairs, count, prev_first):
        u = pos < count[0]
        r = pairs[:, 1] - first_block
        u = u & (r >= 0) & (r < nloc)
        return r, pairs[:, 0] - prev_first, u

    nd, pd, m_nd, m_pd, num, den = lax.optimization_barrier((nd, pd, m_nd, m_pd, num, den))
    sq_nd, _, _ = decode_meta(m_nd, nloc, slots)
    sq_pd, pd_pairs, pd_count = decode_meta(m_pd, nloc, slots)
    pr, pi, pu = prev_entries(pd_pairs, pd_count, first_block - nloc)
    t2 = jnp.concatenate([left, pr])
    s2 = jnp.concatenate([zeros, ones])
    i2 = jnp.concatenate([ridx_dev, pi])
    v2 = jnp.concatenate([used & r_dev, pu])
    tab2 = pack_table(t2, s2, i2, v2, nloc)
    sq2 = jnp.concatenate([sq_nd, sq_pd], axis=0)
    num, den = run_phase("accum", tab2, t2.shape[0], embeddings, sq_col, [nd, pd], sq2, num, den)

    ng, pg, m_ng, m_pg, num, den = lax.optimization_barrier((ng, pg, m_ng, m_pg, num, den))
    sq_ng, _, _ = decode_meta(m_ng, nloc, slots)
    sq_pg, pg_pairs, pg_count = decode_meta(m_pg, nloc, slots)
    gr, gi, gu = prev_entries(pg_pairs, pg_count, first_block - owners * nloc)
    t3 = jnp.concatenate([left, gr])
    s3 = jnp.concatenate([zeros, ones])
    i3 = jnp.concatenate([ridx_grp, gi])
    v3 = jnp.concatenate([used & r_grp, gu])
    tab3 = pack_table(t3, s3, i3, v3, nloc)
    sq3 = jnp.concatenate([sq_ng, sq_pg], axis=0)
    smoothed = run_phase("final", tab3, t3.shape[0], embeddings, sq_col, [ng, pg], sq3, num, den)
    return smoothed.reshape(total_rows, width)


def solution(mesh):
    placed = (P(("group", "dev"), None), P(("group", "dev"), None), P(("group", "dev")))
    return jax.shard_map(
        local, mesh=mesh, in_specs=placed, out_specs=P(("group", "dev"), None), check_vma=False
    )
```
